32 devices in a mesh: groups: 2 (over y), patch: 4 (over z), zbin: 2 (over x), freq: 2 (over core).
Axes of the slice: x: 2, y: 2, z: 4, core: 2. Of those that a mesh axis runs over, the one named last changes fastest.
Arguments:
- density_maps: bfloat16 [8, 4, 1024, 1024], P(('groups', 'patch'), 'zbin', None, 'freq'), parts along dimension 0, may hold values from -6 to 6
- margin_src: int32 [8, 4], P('groups'), parts along dimension 0, may hold values from 0 to 7, as said below
- margin_row: int32 [8, 4], P('groups'), parts along dimension 0, may hold values from 0 to 992
- margin_count: int32 [8], P('groups'), parts along dimension 0, may hold values from 1 to 4
- class_id: int32 [8], P('groups'), parts along dimension 0, may hold values from 0 to 3
- coupling_bank: float32 [4, 128, 128], P('patch'), may hold values from -0.5 to 2
- band_edges: int32 [129], replicated, may hold values from 1 to 511, as said below
Outputs:
- spectra: float32 [8, 10, 128], P(('groups', 'patch'), 'zbin'), parts along dimension 0
The draws below stay inside these ranges and needn't reach their ends.
There are 2 independent parts, one for each index of `groups`. The reference program is written for one: setup_inputs(seed, part) draws one part's arguments, and reference() takes and returns one part's arrays. A program takes and returns all parts, laid end to end along the dimension named above; an argument that names none is the same for every part. Nothing has to cross between parts.
Inputs may be any that keep to these rules, and one draw needn't show every extreme that they name: `margin_src`: entry k of patch p names strip 2 q + s, side s of patch q, where q lies 1 to 1 patches away from p, counted cyclically over the 4 patches. `band_edges`: strictly increasing, the first 1 and the last half of 1024 minus 1.
All inputs are finite; a program needn't handle non-finite values.
Results may differ from the reference program's by a relative error of at most 0.0011.
Values may be sent and summed in bfloat16 or wider, within the bound.
No kernel may reach another device: no remote copies, remote signals or barrier semaphores. Data moves between devices by JAX's collectives and lax.ppermute only.
A program may use at most 64 MiB of HBM per device.

```python
import math
import jax
import jax.numpy as jnp
import numpy as np
from jax import lax

P_SIZE = 1024
BINS = 4
NPAIR = 10
PATCH_DEV = 1
PATCHES = 4
W = 32
APOD = 64
KMAX = 4
NBAND = 128
CLASS_DEV = 1
NCLASS = 4


def draw_density_maps(key, part):
    key = jax.random.fold_in(key, 21)
    key_common, key_own, key_amp = jax.random.split(key, 3)
    log_amp = jax.random.uniform(key_amp, (1, BINS, 1, 1), jnp.float32, math.log(0.5), math.log(2.0))
    amplitude = jnp.exp(log_amp)
    common = jax.random.normal(key_common, (PATCHES, 1, P_SIZE, P_SIZE), jnp.float32)
    own = jax.random.normal(key_own, (PATCHES, BINS, P_SIZE, P_SIZE), jnp.float32)
    field = amplitude * (0.7 * common + 0.7 * own)
    return jnp.clip(field, -6.0, 6.0).astype(jnp.bfloat16)


def draw_margin_src(key, part):
    key = jax.random.fold_in(key, 11)
    key_dist, key_sign, key_side = jax.random.split(key, 3)
    distance = jax.random.randint(key_dist, (PATCHES, KMAX), 1, PATCH_DEV + 1)
    direction = 2 * jax.random.randint(key_sign, (PATCHES, KMAX), 0, 2) - 1
    strip_side = jax.random.randint(key_side, (PATCHES, KMAX), 0, 2)
    distance = distance.at[0, 0].set(PATCH_DEV)
    patch_index = jnp.arange(PATCHES, dtype=jnp.int32)[:, None]
    source = (patch_index + direction * distance) % PATCHES
    return (2 * source + strip_side).astype(jnp.int32)


def draw_margin_row(key, part):
    key = jax.random.fold_in(key, 13)
    rows = jax.random.randint(key, (PATCHES, KMAX), 0, P_SIZE - W + 1)
    rows = rows.at[0, 0].set(0)
    rows = rows.at[PATCHES - 1, 0].set(P_SIZE - W)
    return rows.astype(jnp.int32)


def draw_margin_count(key, part):
    key = jax.random.fold_in(key, 17)
    counts = jax.random.randint(key, (PATCHES,), 1, KMAX + 1)
    counts = counts.at[0].set(KMAX)
    counts = counts.at[PATCHES - 1].set(1)
    return counts.astype(jnp.int32)


def draw_class_id(key, part):
    key = jax.random.fold_in(key, 19)
    key_a, key_b, key_perm, key_pick, key_swap = jax.random.split(key, 5)
    first = jax.random.randint(key_a, (PATCHES,), 0, NCLASS)
    second = jax.random.randint(key_b, (PATCHES,), 0, NCLASS)
    ranked = jnp.minimum(first, second)
    order = jax.random.permutation(key_perm, NCLASS).astype(jnp.int32)
    chosen = jnp.sum(jnp.where(ranked[:, None] == jnp.arange(NCLASS)[None, :], order[None, :], 0), axis=1)
    owners = NCLASS // CLASS_DEV
    patch_pick = jax.random.randint(key_pick, (), 0, PATCHES)
    if PATCHES >= 8:
        device_now = patch_pick // PATCH_DEV
        before = (device_now + owners - 1) % owners * CLASS_DEV
        chosen = chosen.at[patch_pick].set(before)
        other_patch = (patch_pick + PATCHES // 2 + PATCH_DEV) % PATCHES
        other_device = other_patch // PATCH_DEV
        across = (other_device + owners // 2) % owners * CLASS_DEV
        chosen = chosen.at[other_patch].set(across)
    swapped = jax.random.randint(key_swap, (), 0, 2)
    low_value = swapped * (NCLASS - 1)
    high_value = (1 - swapped) * (NCLASS - 1)
    chosen = chosen.at[(patch_pick + 1) % PATCHES].set(low_value)
    chosen = chosen.at[(patch_pick + 2) % PATCHES].set(high_value)
    return chosen.astype(jnp.int32)


def draw_coupling_bank(key, part):
    key = jax.random.fold_in(key, 31)
    key_diag, key_off = jax.random.split(key, 2)
    diagonal = 1.0 + jax.random.uniform(key_diag, (NCLASS, NBAND), jnp.float32, 0.0, 1.0)
    spread = jax.random.normal(key_off, (NCLASS, NBAND, NBAND), jnp.float32) * (0.6 / math.sqrt(NBAND))
    spread = jnp.clip(spread, -0.5, 0.5)
    identity = (jnp.arange(NBAND)[:, None] == jnp.arange(NBAND)[None, :]).astype(jnp.float32)
    return (spread * (1.0 - identity)[None] + diagonal[:, :, None] * identity[None]).astype(jnp.float32)


def draw_band_edges(key, part):
    key = jax.random.fold_in(key, 41)
    inner = jax.random.permutation(key, P_SIZE // 2 - 3) + 2
    chosen = jnp.sort(inner[:NBAND - 1]).astype(jnp.int32)
    first_edge = jnp.array([1], dtype=jnp.int32)
    last_edge = jnp.array([P_SIZE // 2 - 1], dtype=jnp.int32)
    return jnp.concatenate([first_edge, chosen, last_edge])


def setup_inputs(seed: int = 0, part: int = 0) -> dict:
    keys = jax.random.split(jax.random.key(seed), 8)
    own_keys = jax.random.split(jax.random.fold_in(keys[7], part), 8)
    density_maps = draw_density_maps(jax.random.fold_in(jax.random.fold_in(keys[7], part), 71), part)
    margin_src = draw_margin_src(jax.random.fold_in(jax.random.fold_in(keys[7], part), 71), part)
    margin_row = draw_margin_row(jax.random.fold_in(jax.random.fold_in(keys[7], part), 71), part)
    margin_count = draw_margin_count(jax.random.fold_in(jax.random.fold_in(keys[7], part), 71), part)
    class_id = draw_class_id(jax.random.fold_in(jax.random.fold_in(keys[7], part), 71), part)
    coupling_bank = draw_coupling_bank(jax.random.fold_in(keys[7], 71), part)
    band_edges = draw_band_edges(jax.random.fold_in(keys[7], 71), part)
    return dict(density_maps=density_maps, margin_src=margin_src, margin_row=margin_row, margin_count=margin_count, class_id=class_id, coupling_bank=coupling_bank, band_edges=band_edges)


def taper_profile(length, ramp_width):
    position = jnp.arange(length, dtype=jnp.int32)
    distance = jnp.minimum(position, length - 1 - position)
    ramped = 0.5 - 0.5 * jnp.cos(math.pi * (distance.astype(jnp.float32) + 0.5) / ramp_width)
    return jnp.where(distance < ramp_width, ramped, jnp.ones_like(ramped))


def fourier_tables(frequencies, samples, length):
    phases = (frequencies[:, None] * samples[None, :]) % length
    angles = phases.astype(jnp.float32) * (2.0 * math.pi / length)
    return jnp.cos(angles).astype(jnp.bfloat16), jnp.sin(angles).astype(jnp.bfloat16)


def band_table(wave_rows, length, band_edges):
    wave_cols = jnp.arange(length, dtype=jnp.int32)
    folded = jnp.where(wave_cols < length // 2, wave_cols, wave_cols - length)
    radius_squared = (wave_rows[:, None] * wave_rows[:, None] + folded[None, :] * folded[None, :]).reshape(-1)
    edge_squared = band_edges * band_edges
    inside = (radius_squared[:, None] >= edge_squared[None, :-1]) & (radius_squared[:, None] < edge_squared[None, 1:])
    return inside.astype(jnp.float32)


def mode_counts(band_edges, length):
    halfway = length // 2
    wave_rows = jnp.arange(halfway, dtype=jnp.int32)
    wave_abs = jnp.arange(halfway + 1, dtype=jnp.int32)
    weights = jnp.where((wave_abs == 0) | (wave_abs == halfway), 1, 2).astype(jnp.int32)
    radius_squared = wave_rows[:, None] * wave_rows[:, None] + wave_abs[None, :] * wave_abs[None, :]

    def below_edge(edge_value):
        return jnp.sum(jnp.where(radius_squared < edge_value * edge_value, weights[None, :], 0).astype(jnp.int32))

    totals = lax.map(below_edge, band_edges)
    return (totals[1:] - totals[:-1]).astype(jnp.float32)


def rounded(values):
    return lax.optimization_barrier(values.astype(jnp.bfloat16)).astype(jnp.float32)


def reference(density_maps, margin_src, margin_row, margin_count, class_id, coupling_bank, band_edges):
    highest = lax.Precision.HIGHEST
    tops = density_maps[:, :, :W, :]
    bottoms = density_maps[:, :, P_SIZE - W:, :]
    strip_bank = jnp.stack([tops, bottoms], axis=1).reshape(2 * PATCHES, BINS, W, P_SIZE)
    profile = taper_profile(P_SIZE, APOD)
    pixel_index = jnp.arange(P_SIZE, dtype=jnp.int32)
    cos_rows, sin_rows = fourier_tables(jnp.arange(P_SIZE // 2, dtype=jnp.int32), pixel_index, P_SIZE)
    cos_full, sin_full = fourier_tables(pixel_index, pixel_index, P_SIZE)
    cos_rows = cos_rows.astype(jnp.float32)
    sin_rows = sin_rows.astype(jnp.float32)
    cos_full = cos_full.astype(jnp.float32)
    sin_full = sin_full.astype(jnp.float32)
    first_np, second_np = np.triu_indices(BINS)
    first_bin = jnp.asarray(first_np, dtype=jnp.int32)
    second_bin = jnp.asarray(second_np, dtype=jnp.int32)
    counts = mode_counts(band_edges, P_SIZE)
    block_rows = math.gcd(P_SIZE // 2, 16)

    def one_patch(patch_now):
        image = density_maps[patch_now].astype(jnp.float32)
        for entry_index in range(KMAX):
            strip_id = margin_src[patch_now, entry_index]
            live = (entry_index < margin_count[patch_now]).astype(jnp.float32)
            chosen = strip_bank[strip_id].astype(jnp.float32) * live
            row_at = margin_row[patch_now, entry_index].astype(jnp.int32)
            anchor = (jnp.int32(0), row_at, jnp.int32(0))
            current = lax.dynamic_slice(image, anchor, (BINS, W, P_SIZE))
            image = lax.dynamic_update_slice(image, current + chosen, anchor)
        tapered = rounded(image * profile[None, :, None] * profile[None, None, :])
        cols_real = rounded(jnp.einsum("ky,byx->bkx", cos_rows, tapered, precision=highest))
        cols_imag = rounded(-jnp.einsum("ky,byx->bkx", sin_rows, tapered, precision=highest))
        modes_real = rounded(jnp.einsum("bkx,xf->bkf", cols_real, cos_full, precision=highest)
                             + jnp.einsum("bkx,xf->bkf", cols_imag, sin_full, precision=highest))
        modes_imag = rounded(jnp.einsum("bkx,xf->bkf", cols_imag, cos_full, precision=highest)
                             - jnp.einsum("bkx,xf->bkf", cols_real, sin_full, precision=highest))

        def visit_block(running, block_index):
            offset = block_index * block_rows
            real_rows = lax.dynamic_slice_in_dim(modes_real, offset, block_rows, 1)
            imag_rows = lax.dynamic_slice_in_dim(modes_imag, offset, block_rows, 1)
            cross_terms = real_rows[first_bin] * real_rows[second_bin] + imag_rows[first_bin] * imag_rows[second_bin]
            wave_rows = offset + jnp.arange(block_rows, dtype=jnp.int32)
            indicator = band_table(wave_rows, P_SIZE, band_edges)
            summed = jnp.dot(cross_terms.reshape(NPAIR, block_rows * P_SIZE), indicator, precision=highest)
            return running + summed, None

        initial = jnp.zeros((NPAIR, NBAND), jnp.float32)
        totals, unused = lax.scan(visit_block, initial, jnp.arange((P_SIZE // 2) // block_rows, dtype=jnp.int32))
        pseudo = totals / (counts * float(P_SIZE * P_SIZE))[None, :]
        matrix = coupling_bank[class_id[patch_now]]
        return jnp.dot(pseudo, matrix.T, precision=highest)

    return lax.map(one_patch, jnp.arange(PATCHES, dtype=jnp.int32))
```

```python
import math

import jax
import jax.numpy as jnp
import ml_dtypes
import numpy as np
from jax import lax
from jax.experimental import pallas as pl
from jax.experimental.pallas import tpu as pltpu
from jax.sharding import PartitionSpec as P

W = 32
APOD = 64
GROUP = 16


ANY = pl.BlockSpec(memory_space=pl.ANY)
VMEM = pl.BlockSpec(memory_space=pltpu.VMEM)
SMEM = pl.BlockSpec(memory_space=pltpu.SMEM)
BF16 = jnp.bfloat16
F32 = jnp.float32


def taper_of(length):
    position = np.arange(length)
    distance = np.minimum(position, length - 1 - position)
    ramp = 0.5 - 0.5 * np.cos(math.pi * (distance + 0.5) / APOD)
    return np.where(distance < APOD, ramp, 1.0).astype(np.float32)


def trig(frequencies, samples, length):
    phase = (frequencies[:, None] * samples[None, :]) % length
    angle = phase * (2.0 * math.pi / length)
    return np.cos(angle), np.sin(angle)


def row_tables(length, devices):
    half = length // 2
    chunks = half // (2 * GROUP * devices)
    ky = np.arange(half)
    cos_part, sin_part = trig(ky, np.arange(half), length)
    both = np.stack([cos_part, sin_part])
    both = both.reshape(2, chunks, devices, GROUP, 2, half)
    both = both.transpose(1, 4, 2, 0, 3, 5)
    return both.reshape(chunks, 2, devices, 2 * GROUP, half).astype(ml_dtypes.bfloat16)


def column_tables(length):
    half = length // 2
    out = np.zeros((2, half, 2 * half))
    for parity in range(2):
        size = 2 * np.arange(half // 2) + parity
        signed = np.concatenate([size, -size])
        cos_part, sin_part = trig(np.arange(half), signed, length)
        if parity == 0:
            cos_part[:, half // 2] = 0.0
            sin_part[:, half // 2] = 0.0
        out[parity] = np.concatenate([cos_part, sin_part], axis=1)
    return out.astype(ml_dtypes.bfloat16)


def pair_index(first, second, count):
    low = jnp.minimum(first, second)
    high = jnp.maximum(first, second)
    return low * count - (low * (low - 1)) // 2 + high - low


def edge_position(edge_squared, rows_squared):
    gap = jnp.maximum(edge_squared - rows_squared, 0)
    root = jnp.sqrt(gap.astype(F32)).astype(jnp.int32)
    for _ in range(2):
        root = jnp.where(root * root < gap, root + 1, root)
    for _ in range(2):
        less = root - 1
        root = jnp.where((less >= 0) & (less * less >= gap), less, root)
    return root


def gather_kernel(maps, swap, same, cross, sems):
    length = maps.shape[2]
    mine = lax.axis_index("freq")
    other = 1 - mine
    copies = [pltpu.make_async_copy(maps.at[0, other], swap, sems.at[0])]
    for side, start in enumerate((0, length - W)):
        rows = pl.ds(start, W)
        copies.append(
            pltpu.make_async_copy(maps.at[0, mine, rows], same.at[side], sems.at[1 + side])
        )
        copies.append(
            pltpu.make_async_copy(maps.at[0, other, rows], cross.at[side], sems.at[3 + side])
        )
    for copy in copies:
        copy.start()
    for copy in copies:
        copy.wait()


def transform_chunk(table, folded, margin, select, columns_table, cols, outs, sign, zbins, freqs):
    z_at = lax.axis_index("zbin")
    f_at = lax.axis_index("freq")
    devices = zbins * freqs
    half = folded.shape[1]
    rows = devices * 2 * GROUP
    for parity in range(2):
        blocks = []
        for rel in range(devices):
            to_z = lax.rem(z_at + rel // freqs, zbins)
            to_f = lax.rem(f_at + rel % freqs, freqs)
            blocks.append(table[parity, to_z * freqs + to_f])
        left = jnp.concatenate(blocks, axis=0)
        picked = jnp.dot(left, select[parity], preferred_element_type=F32).astype(BF16)
        summed = jnp.dot(left, folded[parity], preferred_element_type=F32)
        summed = summed + jnp.dot(picked, margin[...], preferred_element_type=F32)
        here = slice(parity * rows, (parity + 1) * rows)
        cols[0, here, :] = summed[:, :half].astype(BF16)
        cols[1, here, :] = (summed[:, half:] * sign).astype(BF16)
    for parity in range(2):
        product = jnp.dot(cols[parity], columns_table[parity], preferred_element_type=F32)
        product = product.reshape(2, devices, 2, GROUP, 2 * half)
        real = product[:, :, 0, :, :half] - product[:, :, 1, :, half:]
        imag = product[:, :, 1, :, :half] + product[:, :, 0, :, half:]
        lanes = slice(parity * half, (parity + 1) * half)
        for rel in range(devices):
            for row in range(2):
                here = slice(row * GROUP, (row + 1) * GROUP)
                outs[rel][0, here, lanes] = real[row, rel].astype(BF16)
                outs[rel][1, here, lanes] = imag[row, rel].astype(BF16)


def first_kernel(zbins, freqs, kmax, *refs):
    (maps, other_half, left_same, right_same, left_cross, right_cross, source_ids, source_rows,
     source_counts, row_table, column_table, col_taper, row_taper) = refs[:13]
    devices = zbins * freqs
    outs = refs[13 : 13 + devices]
    folded_out, margin, select = refs[13 + devices : 16 + devices]
    mine, theirs, strips, table, columns, folded, cols, sems = refs[16 + devices :]
    f_at = lax.axis_index("freq")
    p_at = lax.axis_index("patch")
    patches = lax.axis_size("patch")
    length = mine.shape[0]
    half = length // 2
    copies = [
        pltpu.make_async_copy(maps.at[0, f_at], mine, sems.at[0]),
        pltpu.make_async_copy(other_half, theirs, sems.at[1]),
        pltpu.make_async_copy(left_same, strips.at[0, pl.ds(0, 2)], sems.at[2]),
        pltpu.make_async_copy(right_same, strips.at[0, pl.ds(2, 2)], sems.at[3]),
        pltpu.make_async_copy(left_cross, strips.at[1, pl.ds(0, 2)], sems.at[4]),
        pltpu.make_async_copy(right_cross, strips.at[1, pl.ds(2, 2)], sems.at[5]),
        pltpu.make_async_copy(row_table.at[0], table, sems.at[6]),
        pltpu.make_async_copy(column_table, columns, sems.at[7]),
    ]
    for copy in copies:
        copy.start()
    taper_mine = col_taper[pl.ds(f_at, 1), :]
    taper_theirs = col_taper[pl.ds(1 - f_at, 1), :]
    sign = jnp.where(f_at == 0, 1.0, -1.0).astype(F32)

    lane = lax.broadcasted_iota(jnp.int32, (1, kmax * W), 1)
    entry = lane // W
    target = lane - entry * W
    for k in range(kmax):
        target = target + jnp.where(entry == k, source_rows[p_at, k], 0)
    lower = target >= half
    folded_target = jnp.where(lower, target - half, target)
    sample = lax.broadcasted_iota(jnp.int32, (half, kmax * W), 0)
    hit = sample == folded_target
    select[0] = jnp.where(hit, 1.0, 0.0).astype(BF16)
    select[1] = jnp.where(hit, jnp.where(lower, -1.0, 1.0), 0.0).astype(BF16)

    for copy in copies[2:6]:
        copy.wait()
    for k in range(kmax):
        strip = source_ids[p_at, k]
        away = lax.rem(strip // 2 - p_at + patches, patches)
        slot = jnp.where(away == 1, 2, 0) + lax.rem(strip, 2)
        live = jnp.where(k < source_counts[p_at], 1.0, 0.0).astype(F32)
        position = source_rows[p_at, k] + lax.broadcasted_iota(jnp.int32, (W, 128), 0)
        distance = jnp.minimum(position, length - 1 - position)
        ramp = 0.5 - 0.5 * jnp.cos(math.pi * (distance.astype(F32) + 0.5) / APOD)
        weight = jnp.where(distance < APOD, ramp, 1.0) * live
        weight = jnp.tile(weight, (1, half // 128))
        near = strips[0, slot].astype(F32) * taper_mine * weight
        far = strips[1, slot].astype(F32) * taper_theirs * weight
        here = slice(k * W, (k + 1) * W)
        margin[here, :half] = (near + far).astype(BF16)
        margin[here, half:] = (near - far).astype(BF16)

    copies[0].wait()
    copies[1].wait()

    def fold_rows(start, top_taper, low_taper):
        pieces = []
        for offset, taper in ((start, top_taper), (start + half, low_taper)):
            near = mine[pl.ds(offset, GROUP), :].astype(F32) * taper_mine
            far = theirs[pl.ds(offset, GROUP), :].astype(F32) * taper_theirs
            if taper is not None:
                near = near * taper
                far = far * taper
            pieces.append((near + far, near - far))
        (top_even, top_odd), (low_even, low_odd) = pieces
        here = pl.ds(start, GROUP)
        folded[0, here, :half] = (top_even + low_even).astype(BF16)
        folded[0, here, half:] = (top_odd + low_odd).astype(BF16)
        folded[1, here, :half] = (top_even - low_even).astype(BF16)
        folded[1, here, half:] = (top_odd - low_odd).astype(BF16)

    def row_weight(start):
        return jnp.tile(row_taper[pl.ds(start, GROUP), :], (1, half // 128))

    for block in range(APOD // GROUP):
        start = block * GROUP
        fold_rows(start, row_weight(start), None)
        start = half - APOD + block * GROUP
        fold_rows(start, None, row_weight(APOD + block * GROUP))

    def inner(block, carry):
        fold_rows(pl.multiple_of(block * GROUP, GROUP), None, None)
        return carry

    lax.fori_loop(APOD // GROUP, (half - APOD) // GROUP, inner, 0)
    keep = pltpu.make_async_copy(folded, folded_out, sems.at[8])
    keep.start()
    copies[6].wait()
    copies[7].wait()
    transform_chunk(table, folded, margin, select, columns, cols, outs, sign, zbins, freqs)
    keep.wait()


def later_kernel(zbins, freqs, chunks, *refs):
    row_table, column_table, folded_in, margin, select = refs[:5]
    devices = zbins * freqs
    outs = refs[5 : 5 + (chunks - 1) * devices]
    table, columns, folded, cols, sems = refs[5 + (chunks - 1) * devices :]
    copies = [
        pltpu.make_async_copy(row_table.at[pl.ds(1, chunks - 1)], table, sems.at[0]),
        pltpu.make_async_copy(folded_in, folded, sems.at[1]),
        pltpu.make_async_copy(column_table, columns, sems.at[2]),
    ]
    for copy in copies:
        copy.start()
    sign = jnp.where(lax.axis_index("freq") == 0, 1.0, -1.0).astype(F32)
    for copy in copies:
        copy.wait()
    for chunk in range(chunks - 1):
        transform_chunk(
            table.at[chunk], folded, margin, select, columns, cols,
            outs[chunk * devices : (chunk + 1) * devices], sign, zbins, freqs,
        )


def band_kernel(zbins, freqs, chunk, chunks, per, *refs):
    devices = zbins * freqs
    edges = refs[0]
    modes = refs[1 : 1 + devices]
    rest = refs[1 + devices :]
    earlier = None
    if chunk > 0:
        earlier, rest = rest[0], rest[1:]
    running, rest = rest[0], rest[1:]
    count_out = placed = None
    if chunk == 0:
        count_out, rest = rest[0], rest[1:]
    if chunk == chunks - 1:
        placed, rest = rest[0], rest[1:]
    upper, lower = rest
    z_at = lax.axis_index("zbin")
    f_at = lax.axis_index("freq")
    own = z_at * freqs + f_at
    half = modes[0].shape[2] // 2
    quarter = half // 2
    rows = 2 * GROUP
    bands = edges.shape[1]
    pairs = [(a, b) for a in range(devices) for b in range(a, devices)]
    for row in range(2):
        here = slice(row * GROUP, (row + 1) * GROUP)
        for block in range(half // 128):
            parity, at = divmod(block * 128, quarter)
            plus = slice(parity * half + at, parity * half + at + 128)
            minus = slice(plus.start + quarter, plus.stop + quarter)
            loaded = [
                [m[part, here, lanes].astype(F32) for lanes in (plus, minus) for part in (0, 1)]
                for m in modes
            ]
            if chunk == 0 and row == 0 and block == 0:
                zero = (
                    (lax.broadcasted_iota(jnp.int32, (GROUP, 128), 0) == 0)
                    & (lax.broadcasted_iota(jnp.int32, (GROUP, 128), 1) == 0)
                    & (own == 0)
                )
                loaded = [
                    [jnp.where(zero, 0.0, v) for v in parts[:2]] + parts[2:] for parts in loaded
                ]
            for number, (a, b) in enumerate(pairs):
                total = loaded[a][0] * loaded[b][0]
                for part in range(1, 4):
                    total = total + loaded[a][part] * loaded[b][part]
                high = total.astype(BF16)
                low = (total - high.astype(F32)).astype(BF16)
                at_rows = slice(number * rows + row * GROUP, number * rows + (row + 1) * GROUP)
                lanes = slice(block * 128, (block + 1) * 128)
                upper[at_rows, lanes] = high
                lower[at_rows, lanes] = low
    lane = lax.broadcasted_iota(jnp.int32, (half, half), 0)
    size = jnp.where(lane < quarter, 2 * lane, 2 * (lane - quarter) + 1)
    limit = lax.broadcasted_iota(jnp.int32, (half, half), 1)
    below = jnp.where(size < limit, 1.0, 0.0).astype(BF16)
    sums = jnp.dot(upper[...], below, preferred_element_type=F32) + jnp.dot(
        lower[...], below, preferred_element_type=F32
    )
    edge = edges[...]
    row_at = lax.broadcasted_iota(jnp.int32, (rows, bands), 0)
    within = jnp.where(row_at < GROUP, 2 * row_at, 2 * (row_at - GROUP) + 1)
    ky = (chunk * devices + own) * rows + within
    place = edge_position(edge * edge, ky * ky)
    tile = place // 128
    inside = place - tile * 128
    for number in range(len(pairs)):
        here = slice(number * rows, (number + 1) * rows)
        chosen = jnp.zeros((rows, bands), F32)
        for block in range(half // 128):
            part = sums[here, block * 128 : (block + 1) * 128]
            moved = jnp.take_along_axis(part, inside, axis=1)
            chosen = jnp.where(tile == block, moved, chosen)
        part = jnp.sum(chosen.reshape(rows // 8, 8, bands), axis=0)
        if earlier is not None:
            part = part + earlier[number]
        running[number] = part
    if count_out is not None:
        wave = lax.broadcasted_iota(jnp.int32, (half, bands), 0)
        position = edge_position(edge * edge, wave * wave)
        inside_row = jnp.where(position > 0, 2 * position - 1, 0).astype(F32)
        below_edge = jnp.sum(inside_row, axis=0, keepdims=True)
        previous = pltpu.roll(jnp.broadcast_to(below_edge, (8, bands)), 1, axis=1)
        first = lax.broadcasted_iota(jnp.int32, (8, bands), 1) == 0
        count_out[...] = below_edge - jnp.where(first, 1.0, previous)
    if placed is not None:
        first_np, second_np = np.triu_indices(devices)

        def place_of(number):
            source = int(number)
            rel_z = lax.rem(z_at - source // freqs + zbins, zbins)
            rel_f = lax.rem(f_at - source % freqs + freqs, freqs)
            return rel_z * freqs + rel_f

        for number in range(len(pairs)):
            low = place_of(first_np[number])
            high = place_of(second_np[number])
            row = jnp.sum(running[pair_index(low, high, devices)], axis=0, keepdims=True)
            placed[number // per, pl.ds(number % per, 1), :] = row


def final_kernel(count, *refs):
    parts = refs[:count]
    modes, bank, class_id, out, matrix, sem = refs[count:]
    z_at = lax.axis_index("zbin")
    p_at = lax.axis_index("patch")
    slot = class_id[p_at] ^ p_at
    copy = pltpu.make_async_copy(bank.at[slot], matrix, sem)
    copy.start()
    total = parts[0][z_at]
    for part in parts[1:]:
        total = total + part[z_at]
    rows, bands = total.shape
    first = lax.broadcasted_iota(jnp.int32, (rows, bands), 1) == 0
    total = total - jnp.where(first, 0.0, pltpu.roll(total, 1, axis=1))
    pseudo = total / modes[0:1, :]
    copy.wait()
    spectra = lax.dot_general(
        pseudo, matrix[...], (((1,), (1,)), ((), ())),
        precision=lax.Precision.HIGHEST, preferred_element_type=F32,
    )
    out[0] = spectra[: out.shape[1]]


def per_device(
    density_maps, margin_src, margin_row, margin_count, class_id, coupling_bank, band_edges
):
    patch_local, bins_local, length, columns = density_maps.shape
    freqs = lax.axis_size("freq")
    zbins = lax.axis_size("zbin")
    patches = lax.axis_size("patch")
    devices = zbins * freqs
    half = length // 2
    kmax = margin_src.shape[1]
    bands = band_edges.shape[0] - 1
    chunks = half // (2 * GROUP * devices)
    rows = 2 * GROUP
    assert patch_local == 1 and bins_local == freqs == 2 and columns == half and chunks >= 2
    assert patches & (patches - 1) == 0
    pairs = devices * (devices + 1) // 2
    per = pairs // zbins
    padded = -(-per // 8) * 8
    shape = jax.ShapeDtypeStruct
    dma = pltpu.SemaphoreType.DMA

    swap, same, cross = pl.pallas_call(
        gather_kernel,
        in_specs=[ANY],
        out_specs=[ANY] * 3,
        out_shape=[
            shape((length, columns), BF16), shape((2, W, columns), BF16),
            shape((2, W, columns), BF16),
        ],
        scratch_shapes=[dma((5,))],
        name="gather",
    )(density_maps)
    theirs = lax.ppermute(swap, "freq", [(0, 1), (1, 0)])
    ahead = [(i, (i + 1) % patches) for i in range(patches)]
    behind = [(b, a) for a, b in ahead]
    crossed = [
        [(a * freqs + f, b * freqs + 1 - f) for a, b in hops for f in range(freqs)]
        for hops in (ahead, behind)
    ]
    left_same = lax.ppermute(same, "patch", ahead)
    right_same = lax.ppermute(same, "patch", behind)
    left_cross = lax.ppermute(cross, ("patch", "freq"), crossed[0])
    right_cross = lax.ppermute(cross, ("patch", "freq"), crossed[1])

    row_table = jnp.asarray(row_tables(length, devices))
    column_table = jnp.asarray(column_tables(length))
    profile = taper_of(length)
    col_taper = jnp.asarray(profile.reshape(2, half))
    edge_rows = np.concatenate([profile[:APOD], profile[length - APOD :]])
    row_taper = jnp.asarray(np.broadcast_to(edge_rows[:, None], (2 * APOD, 128)).copy())
    piece = shape((2, rows, length), BF16)
    cols = pltpu.VMEM((2, 2 * devices * rows, half), BF16)
    result = pl.pallas_call(
        lambda *refs: first_kernel(zbins, freqs, kmax, *refs),
        in_specs=[ANY] * 6 + [SMEM] * 3 + [ANY] * 2 + [VMEM] * 2,
        out_specs=[VMEM] * devices + [ANY, VMEM, VMEM],
        out_shape=[piece] * devices + [
            shape((2, half, length), BF16), shape((kmax * W, length), BF16),
            shape((2, half, kmax * W), BF16),
        ],
        scratch_shapes=[
            pltpu.VMEM((length, half), BF16), pltpu.VMEM((length, half), BF16),
            pltpu.VMEM((2, 4, W, half), BF16), pltpu.VMEM(row_table.shape[1:], BF16),
            pltpu.VMEM(column_table.shape, BF16), pltpu.VMEM((2, half, length), BF16),
            cols, dma((9,)),
        ],
        name="first",
    )(
        density_maps, theirs, left_same, right_same, left_cross, right_cross, margin_src,
        margin_row, margin_count, row_table, column_table, col_taper, row_taper,
    )
    pieces = [result[:devices]]
    folded, margin, select = result[devices:]
    later = pl.pallas_call(
        lambda *refs: later_kernel(zbins, freqs, chunks, *refs),
        in_specs=[ANY] * 3 + [VMEM] * 2,
        out_specs=[VMEM] * (devices * (chunks - 1)),
        out_shape=[piece] * (devices * (chunks - 1)),
        scratch_shapes=[
            pltpu.VMEM((chunks - 1,) + row_table.shape[1:], BF16),
            pltpu.VMEM(column_table.shape, BF16), pltpu.VMEM((2, half, length), BF16),
            cols, dma((3,)),
        ],
        name="later",
    )(row_table, column_table, folded, margin, select)
    for chunk in range(chunks - 1):
        pieces.append(later[chunk * devices : (chunk + 1) * devices])

    hops = []
    for rel in range(devices):
        hops.append([
            (z * freqs + f,
             (z + rel // freqs) % zbins * freqs + (f + rel % freqs) % freqs)
            for z in range(zbins) for f in range(freqs)
        ])
    received = []
    for group in pieces:
        received.append(
            [group[0]]
            + [lax.ppermute(group[rel], ("zbin", "freq"), hops[rel]) for rel in range(1, devices)]
        )

    bank = coupling_bank
    step = 1
    while step < patches:
        bank = jnp.concatenate(
            [bank, lax.ppermute(bank, "patch", [(i, i ^ step) for i in range(patches)])], axis=0
        )
        step *= 2

    upper_edges = band_edges[1:].reshape(1, bands)
    running = None
    for chunk in range(chunks):
        out_shape = [shape((pairs, 8, bands), F32)]
        if chunk == 0:
            out_shape.append(shape((8, bands), F32))
        if chunk == chunks - 1:
            out_shape.append(shape((zbins, padded, bands), F32))
        arrays = [upper_edges] + received[chunk] + ([running] if chunk > 0 else [])
        got = pl.pallas_call(
            lambda *refs, chunk=chunk: band_kernel(zbins, freqs, chunk, chunks, per, *refs),
            in_specs=[VMEM] * len(arrays),
            out_specs=[VMEM] * len(out_shape),
            out_shape=out_shape,
            scratch_shapes=[pltpu.VMEM((pairs * rows, half), BF16)] * 2,
            name="bands" + str(chunk),
        )(*arrays)
        running = got[0]
        if chunk == 0:
            counts = got[1]
        if chunk == chunks - 1:
            placed = got[-1]
    counts = counts * float(length * length)
    parts = [placed] + [
        lax.ppermute(placed, ("zbin", "freq"), hops[rel]) for rel in range(1, devices)
    ]
    return pl.pallas_call(
        lambda *refs: final_kernel(devices, *refs),
        in_specs=[VMEM] * (devices + 1) + [ANY, SMEM],
        out_specs=VMEM,
        out_shape=shape((1, per, bands), F32),
        scratch_shapes=[pltpu.VMEM((bands, bands), F32), dma(())],
        name="final",
    )(*parts, counts, bank, class_id)


def solution(mesh):
    in_specs = (
        P(("groups", "patch"), "zbin", None, "freq"),
        P("groups", None),
        P("groups", None),
        P("groups"),
        P("groups"),
        P("patch", None, None),
        P(),
    )
    out_specs = P(("groups", "patch"), "zbin", None)
    return jax.shard_map(
        per_device, mesh=mesh, in_specs=in_specs, out_specs=out_specs, check_vma=False
    )
```

```python
import math

import jax
import jax.numpy as jnp
import ml_dtypes
import numpy as np
from jax import lax
from jax.experimental import pallas as pl
from jax.experimental.pallas import tpu as pltpu
from jax.sharding import PartitionSpec as P

W = 32
APOD = 64
GROUP = 16


HBM = pl.BlockSpec(memory_space=pltpu.HBM)
VMEM = pl.BlockSpec(memory_space=pltpu.VMEM)
SMEM = pl.BlockSpec(memory_space=pltpu.SMEM)
BF16 = jnp.bfloat16
F32 = jnp.float32


def taper_of(length):
    position = np.arange(length)
    distance = np.minimum(position, length - 1 - position)
    ramp = 0.5 - 0.5 * np.cos(math.pi * (distance + 0.5) / APOD)
    return np.where(distance < APOD, ramp, 1.0).astype(np.float32)


def trig(frequencies, samples, length):
    phase = (frequencies[:, None] * samples[None, :]) % length
    angle = phase * (2.0 * math.pi / length)
    return np.cos(angle), np.sin(angle)


def row_tables(length, devices):
    half = length // 2
    chunks = half // (2 * GROUP * devices)
    ky = np.arange(half)
    cos_part, sin_part = trig(ky, np.arange(half), length)
    both = np.stack([cos_part, sin_part])
    both = both.reshape(2, chunks, devices, GROUP, 2, half)
    both = both.transpose(1, 4, 2, 0, 3, 5)
    return both.reshape(chunks, 2, devices, 2 * GROUP, half).astype(ml_dtypes.bfloat16)


def column_tables(length):
    half = length // 2
    out = np.zeros((2, half, 2 * half))
    for parity in range(2):
        size = 2 * np.arange(half // 2) + parity
        signed = np.concatenate([size, -size])
        cos_part, sin_part = trig(np.arange(half), signed, length)
        if parity == 0:
            cos_part[:, half // 2] = 0.0
            sin_part[:, half // 2] = 0.0
        out[parity] = np.concatenate([cos_part, sin_part], axis=1)
    return out.astype(ml_dtypes.bfloat16)


def pair_index(first, second, count):
    low = jnp.minimum(first, second)
    high = jnp.maximum(first, second)
    return low * count - (low * (low - 1)) // 2 + high - low


def edge_position(edge_squared, rows_squared):
    gap = jnp.maximum(edge_squared - rows_squared, 0)
    root = jnp.sqrt(gap.astype(F32)).astype(jnp.int32)
    for _ in range(2):
        root = jnp.where(root * root < gap, root + 1, root)
    for _ in range(2):
        less = root - 1
        root = jnp.where((less >= 0) & (less * less >= gap), less, root)
    return root


def gather_kernel(maps, swap, mine, same, cross, sems):
    length = maps.shape[2]
    here = lax.axis_index("freq")
    other = 1 - here
    copies = [
        pltpu.make_async_copy(maps.at[0, other], swap, sems.at[0]),
        pltpu.make_async_copy(maps.at[0, here], mine, sems.at[1]),
    ]
    for side, start in enumerate((0, length - W)):
        rows = pl.ds(start, W)
        copies.append(
            pltpu.make_async_copy(maps.at[0, here, rows], same.at[side], sems.at[2 + side])
        )
        copies.append(
            pltpu.make_async_copy(maps.at[0, other, rows], cross.at[side], sems.at[4 + side])
        )
    for copy in copies:
        copy.start()
    for copy in copies:
        copy.wait()


def transform(tables, folded, margin, select, columns_table, cols, outs, sign, zbins, freqs):
    z_at = lax.axis_index("zbin")
    f_at = lax.axis_index("freq")
    devices = zbins * freqs
    chunks = len(tables)
    half = folded.shape[1]
    rows = chunks * devices * 2 * GROUP
    for parity in range(2):
        blocks = []
        for table in tables:
            for rel in range(devices):
                to_z = lax.rem(z_at + rel // freqs, zbins)
                to_f = lax.rem(f_at + rel % freqs, freqs)
                blocks.append(table[parity, to_z * freqs + to_f])
        left = jnp.concatenate(blocks, axis=0)
        picked = jnp.dot(left, select[parity], preferred_element_type=F32).astype(BF16)
        summed = jnp.dot(left, folded[parity], preferred_element_type=F32)
        summed = summed + jnp.dot(picked, margin[...], preferred_element_type=F32)
        here = slice(parity * rows, (parity + 1) * rows)
        cols[0, here, :] = summed[:, :half].astype(BF16)
        cols[1, here, :] = (summed[:, half:] * sign).astype(BF16)
    for parity in range(2):
        product = jnp.dot(cols[parity], columns_table[parity], preferred_element_type=F32)
        product = product.reshape(2, chunks * devices, 2, GROUP, 2 * half)
        real = product[:, :, 0, :, :half] - product[:, :, 1, :, half:]
        imag = product[:, :, 1, :, :half] + product[:, :, 0, :, half:]
        lanes = slice(parity * half, (parity + 1) * half)
        for rel in range(chunks * devices):
            for row in range(2):
                here = slice(row * GROUP, (row + 1) * GROUP)
                outs[rel][0, here, lanes] = real[row, rel].astype(BF16)
                outs[rel][1, here, lanes] = imag[row, rel].astype(BF16)


def first_kernel(zbins, freqs, kmax, *refs):
    (mine, theirs, left_same, right_same, left_cross, right_cross, source_ids, source_rows,
     source_counts, row_table, columns, col_taper, row_taper) = refs[:13]
    devices = zbins * freqs
    outs = refs[13 : 13 + devices]
    folded, margin, select = refs[13 + devices : 16 + devices]
    strips, cols = refs[16 + devices :]
    f_at = lax.axis_index("freq")
    p_at = lax.axis_index("patch")
    length = mine.shape[0]
    half = length // 2
    strips[0, 0:2] = left_same[...]
    strips[0, 2:4] = right_same[...]
    strips[1, 0:2] = left_cross[...]
    strips[1, 2:4] = right_cross[...]
    taper_mine = col_taper[pl.ds(f_at, 1), :]
    taper_theirs = col_taper[pl.ds(1 - f_at, 1), :]
    sign = jnp.where(f_at == 0, 1.0, -1.0).astype(F32)

    lane = lax.broadcasted_iota(jnp.int32, (1, kmax * W), 1)
    entry = lane // W
    target = lane - entry * W
    for k in range(kmax):
        target = target + jnp.where(entry == k, source_rows[p_at, k], 0)
    lower = target >= half
    folded_target = jnp.where(lower, target - half, target)
    sample = lax.broadcasted_iota(jnp.int32, (half, kmax * W), 0)
    hit = sample == folded_target
    select[0] = jnp.where(hit, 1.0, 0.0).astype(BF16)
    select[1] = jnp.where(hit, jnp.where(lower, -1.0, 1.0), 0.0).astype(BF16)

    for k in range(kmax):
        strip = source_ids[p_at, k]
        near_pair = strip // 2 == p_at + 1 - 2 * lax.rem(p_at, 2)
        slot = jnp.where(near_pair, 0, 2) + lax.rem(strip, 2)
        live = jnp.where(k < source_counts[p_at], 1.0, 0.0).astype(F32)
        position = source_rows[p_at, k] + lax.broadcasted_iota(jnp.int32, (W, 128), 0)
        distance = jnp.minimum(position, length - 1 - position)
        ramp = 0.5 - 0.5 * jnp.cos(math.pi * (distance.astype(F32) + 0.5) / APOD)
        weight = jnp.where(distance < APOD, ramp, 1.0) * live
        weight = jnp.tile(weight, (1, half // 128))
        near = strips[0, slot].astype(F32) * taper_mine * weight
        far = strips[1, slot].astype(F32) * taper_theirs * weight
        here = slice(k * W, (k + 1) * W)
        margin[here, :half] = (near + far).astype(BF16)
        margin[here, half:] = (near - far).astype(BF16)

    def fold_rows(start, top_taper, low_taper):
        pieces = []
        for offset, taper in ((start, top_taper), (start + half, low_taper)):
            near = mine[pl.ds(offset, GROUP), :].astype(F32) * taper_mine
            far = theirs[pl.ds(offset, GROUP), :].astype(F32) * taper_theirs
            if taper is not None:
                near = near * taper
                far = far * taper
            pieces.append((near + far, near - far))
        (top_even, top_odd), (low_even, low_odd) = pieces
        here = pl.ds(start, GROUP)
        folded[0, here, :half] = (top_even + low_even).astype(BF16)
        folded[0, here, half:] = (top_odd + low_odd).astype(BF16)
        folded[1, here, :half] = (top_even - low_even).astype(BF16)
        folded[1, here, half:] = (top_odd - low_odd).astype(BF16)

    def row_weight(start):
        return jnp.tile(row_taper[pl.ds(start, GROUP), :], (1, half // 128))

    for block in range(APOD // GROUP):
        start = block * GROUP
        fold_rows(start, row_weight(start), None)
        start = half - APOD + block * GROUP
        fold_rows(start, None, row_weight(APOD + block * GROUP))

    def inner(block, carry):
        fold_rows(pl.multiple_of(block * GROUP, GROUP), None, None)
        return carry

    lax.fori_loop(APOD // GROUP, (half - APOD) // GROUP, inner, 0)
    transform([row_table.at[0]], folded, margin, select, columns, cols, outs, sign, zbins, freqs)


def later_kernel(zbins, freqs, chunks, *refs):
    row_table, columns, folded, margin, select = refs[:5]
    outs = refs[5:-1]
    cols = refs[-1]
    sign = jnp.where(lax.axis_index("freq") == 0, 1.0, -1.0).astype(F32)
    tables = [row_table.at[chunk] for chunk in range(chunks - 1)]
    transform(tables, folded, margin, select, columns, cols, outs, sign, zbins, freqs)


def band_kernel(zbins, freqs, chunk, chunks, per, *refs):
    devices = zbins * freqs
    edges = refs[0]
    modes = refs[1 : 1 + devices]
    rest = refs[1 + devices :]
    earlier = None
    if chunk > 0:
        earlier, rest = rest[0], rest[1:]
    if chunk == chunks - 1:
        counts, bank, class_id = rest[:3]
        results, rest = rest[3 : 3 + devices], rest[3 + devices :]
        running, placed, rest = rest[0], rest[1], rest[2:]
    else:
        running, rest = rest[0], rest[1:]
    count_out = None
    if chunk == 0:
        count_out, rest = rest[0], rest[1:]
    upper, lower = rest
    z_at = lax.axis_index("zbin")
    f_at = lax.axis_index("freq")
    own = z_at * freqs + f_at
    half = modes[0].shape[2] // 2
    quarter = half // 2
    rows = 2 * GROUP
    bands = edges.shape[1]
    pairs = [(a, b) for a in range(devices) for b in range(a, devices)]
    for row in range(2):
        here = slice(row * GROUP, (row + 1) * GROUP)
        for block in range(half // 128):
            parity, at = divmod(block * 128, quarter)
            plus = slice(parity * half + at, parity * half + at + 128)
            minus = slice(plus.start + quarter, plus.stop + quarter)
            loaded = [
                [m[part, here, lanes].astype(F32) for lanes in (plus, minus) for part in (0, 1)]
                for m in modes
            ]
            if chunk == 0 and row == 0 and block == 0:
                zero = (
                    (lax.broadcasted_iota(jnp.int32, (GROUP, 128), 0) == 0)
                    & (lax.broadcasted_iota(jnp.int32, (GROUP, 128), 1) == 0)
                    & (own == 0)
                )
                loaded = [
                    [jnp.where(zero, 0.0, v) for v in parts[:2]] + parts[2:] for parts in loaded
                ]
            for number, (a, b) in enumerate(pairs):
                total = loaded[a][0] * loaded[b][0]
                for part in range(1, 4):
                    total = total + loaded[a][part] * loaded[b][part]
                high = total.astype(BF16)
                low = (total - high.astype(F32)).astype(BF16)
                at_rows = slice(number * rows + row * GROUP, number * rows + (row + 1) * GROUP)
                lanes = slice(block * 128, (block + 1) * 128)
                upper[at_rows, lanes] = high
                lower[at_rows, lanes] = low
    lane = lax.broadcasted_iota(jnp.int32, (half, half), 0)
    size = jnp.where(lane < quarter, 2 * lane, 2 * (lane - quarter) + 1)
    limit = lax.broadcasted_iota(jnp.int32, (half, half), 1)
    below = jnp.where(size < limit, 1.0, 0.0).astype(BF16)
    sums = jnp.dot(upper[...], below, preferred_element_type=F32) + jnp.dot(
        lower[...], below, preferred_element_type=F32
    )
    edge = edges[...]
    row_at = lax.broadcasted_iota(jnp.int32, (rows, bands), 0)
    within = jnp.where(row_at < GROUP, 2 * row_at, 2 * (row_at - GROUP) + 1)
    ky = (chunk * devices + own) * rows + within
    place = edge_position(edge * edge, ky * ky)
    tile = place // 128
    inside = place - tile * 128
    for number in range(len(pairs)):
        here = slice(number * rows, (number + 1) * rows)
        chosen = jnp.zeros((rows, bands), F32)
        for block in range(half // 128):
            part = sums[here, block * 128 : (block + 1) * 128]
            moved = jnp.take_along_axis(part, inside, axis=1)
            chosen = jnp.where(tile == block, moved, chosen)
        part = jnp.sum(chosen.reshape(rows // 8, 8, bands), axis=0)
        if earlier is not None:
            part = part + earlier[number]
        running[number] = part
    if count_out is not None:
        wave = lax.broadcasted_iota(jnp.int32, (half, bands), 0)
        position = edge_position(edge * edge, wave * wave)
        inside_row = jnp.where(position > 0, 2 * position - 1, 0).astype(F32)
        below_edge = jnp.sum(inside_row, axis=0, keepdims=True)
        previous = pltpu.roll(jnp.broadcast_to(below_edge, (8, bands)), 1, axis=1)
        first = lax.broadcasted_iota(jnp.int32, (8, bands), 1) == 0
        count_out[...] = (below_edge - jnp.where(first, 1.0, previous)) * float(4 * half * half)
    if chunk == chunks - 1:
        first_np, second_np = np.triu_indices(devices)

        def place_of(number):
            source = int(number)
            rel_z = lax.rem(z_at - source // freqs + zbins, zbins)
            rel_f = lax.rem(f_at - source % freqs + freqs, freqs)
            return rel_z * freqs + rel_f

        for number in range(len(pairs)):
            low = place_of(first_np[number])
            high = place_of(second_np[number])
            row = jnp.sum(running[pair_index(low, high, devices)], axis=0, keepdims=True)
            placed[pl.ds(number, 1), :] = row
        total = placed[...]
        first = lax.broadcasted_iota(jnp.int32, total.shape, 1) == 0
        total = total - jnp.where(first, 0.0, pltpu.roll(total, 1, axis=1))
        pseudo = total / counts[0:1, :]
        p_at = lax.axis_index("patch")
        spectra = lax.dot_general(
            pseudo, bank[class_id[p_at] ^ p_at], (((1,), (1,)), ((), ())),
            precision=lax.Precision.HIGHEST, preferred_element_type=F32,
        )
        placed[...] = spectra
        for rel in range(devices):
            to_z = lax.rem(z_at + rel // freqs, zbins)
            for number in range(per):
                results[rel][number] = placed[pl.ds(to_z * per + number, 1), :]


def per_device(
    density_maps, margin_src, margin_row, margin_count, class_id, coupling_bank, band_edges
):
    patch_local, bins_local, length, columns = density_maps.shape
    freqs = lax.axis_size("freq")
    zbins = lax.axis_size("zbin")
    patches = lax.axis_size("patch")
    devices = zbins * freqs
    half = length // 2
    kmax = margin_src.shape[1]
    bands = band_edges.shape[0] - 1
    chunks = half // (2 * GROUP * devices)
    rows = 2 * GROUP
    assert patch_local == 1 and bins_local == freqs == 2 and columns == half and chunks >= 2
    assert patches & (patches - 1) == 0
    pairs = devices * (devices + 1) // 2
    per = pairs // zbins
    padded = -(-pairs // 8) * 8
    shape = jax.ShapeDtypeStruct

    def limit(megabytes):
        return pltpu.CompilerParams(vmem_limit_bytes=megabytes << 20)

    swap, mine, same, cross = pl.pallas_call(
        gather_kernel,
        in_specs=[HBM],
        out_specs=[VMEM] * 4,
        out_shape=[shape((length, columns), BF16)] * 2 + [shape((2, W, columns), BF16)] * 2,
        scratch_shapes=[pltpu.SemaphoreType.DMA((6,))],
        compiler_params=limit(6),
        name="gather",
    )(density_maps)
    theirs = lax.ppermute(swap, "freq", [(0, 1), (1, 0)])
    matchings = [
        [(p, p ^ 1) for p in range(patches)],
        [(p, (p - 1 + 2 * (p % 2)) % patches) for p in range(patches)],
    ]
    arrived = []
    for hops in matchings:
        crossed = [(a * freqs + f, b * freqs + 1 - f) for a, b in hops for f in range(freqs)]
        arrived.append(lax.ppermute(same, "patch", hops))
        arrived.append(lax.ppermute(cross, ("patch", "freq"), crossed))
    left_same, left_cross, right_same, right_cross = arrived

    row_table = row_tables(length, devices)
    first_table, later_table = jnp.asarray(row_table[:1]), jnp.asarray(row_table[1:])
    column_table = jnp.asarray(column_tables(length))
    profile = taper_of(length)
    col_taper = jnp.asarray(profile.reshape(2, half))
    edge_rows = np.concatenate([profile[:APOD], profile[length - APOD :]])
    row_taper = jnp.asarray(np.broadcast_to(edge_rows[:, None], (2 * APOD, 128)).copy())
    piece = shape((2, rows, length), BF16)
    result = pl.pallas_call(
        lambda *refs: first_kernel(zbins, freqs, kmax, *refs),
        in_specs=[VMEM] * 6 + [SMEM] * 3 + [VMEM] * 4,
        out_specs=[VMEM] * (devices + 3),
        out_shape=[piece] * devices + [
            shape((2, half, length), BF16), shape((kmax * W, length), BF16),
            shape((2, half, kmax * W), BF16),
        ],
        scratch_shapes=[
            pltpu.VMEM((2, 4, W, half), BF16), pltpu.VMEM((2, 2 * devices * rows, half), BF16),
        ],
        compiler_params=limit(24),
        name="first",
    )(
        mine, theirs, left_same, right_same, left_cross, right_cross, margin_src,
        margin_row, margin_count, first_table, column_table, col_taper, row_taper,
    )
    pieces = [result[:devices]]
    folded, margin, select = result[devices:]
    later = pl.pallas_call(
        lambda *refs: later_kernel(zbins, freqs, chunks, *refs),
        in_specs=[VMEM] * 5,
        out_specs=[VMEM] * (devices * (chunks - 1)),
        out_shape=[piece] * (devices * (chunks - 1)),
        scratch_shapes=[pltpu.VMEM((2, 2 * (chunks - 1) * devices * rows, half), BF16)],
        compiler_params=limit(32),
        name="later",
    )(later_table, column_table, folded, margin, select)
    for chunk in range(chunks - 1):
        pieces.append(later[chunk * devices : (chunk + 1) * devices])

    hops = []
    for rel in range(devices):
        hops.append([
            (z * freqs + f,
             (z + rel // freqs) % zbins * freqs + (f + rel % freqs) % freqs)
            for z in range(zbins) for f in range(freqs)
        ])
    received = []
    for group in pieces:
        received.append(
            [group[0]]
            + [lax.ppermute(group[rel], ("zbin", "freq"), hops[rel]) for rel in range(1, devices)]
        )

    bank = coupling_bank
    step = 1
    while step < patches:
        bank = jnp.concatenate(
            [bank, lax.ppermute(bank, "patch", [(i, i ^ step) for i in range(patches)])], axis=0
        )
        step *= 2

    upper_edges = band_edges[1:].reshape(1, bands)
    running = None
    for chunk in range(chunks):
        arrays = [upper_edges] + received[chunk] + ([running] if chunk > 0 else [])
        specs = [VMEM] * len(arrays)
        scratch = [pltpu.VMEM((pairs * rows, half), BF16)] * 2
        sums = (pairs, 8, bands)
        if chunk < chunks - 1:
            out_shape = [shape(sums, F32)]
            if chunk == 0:
                out_shape.append(shape((8, bands), F32))
        else:
            arrays += [counts, bank, class_id]
            specs += [VMEM, VMEM, SMEM]
            out_shape = [shape((per, 1, bands), F32)] * devices
            scratch = [pltpu.VMEM(sums, F32), pltpu.VMEM((padded, bands), F32)] + scratch
        got = pl.pallas_call(
            lambda *refs, chunk=chunk: band_kernel(zbins, freqs, chunk, chunks, per, *refs),
            in_specs=specs,
            out_specs=[VMEM] * len(out_shape),
            out_shape=out_shape,
            scratch_shapes=scratch,
            compiler_params=limit(8),
            name="bands" + str(chunk),
        )(*arrays)
        if chunk < chunks - 1:
            running = got[0]
        if chunk == 0:
            counts = got[1]
    total = got[0]
    for rel in range(1, devices):
        total = total + lax.ppermute(got[rel], ("zbin", "freq"), hops[rel])
    return total.reshape(patch_local, per, bands)


def solution(mesh):
    in_specs = (
        P(("groups", "patch"), "zbin", None, "freq"),
        P("groups", None),
        P("groups", None),
        P("groups"),
        P("groups"),
        P("patch", None, None),
        P(),
    )
    out_specs = P(("groups", "patch"), "zbin", None)
    return jax.shard_map(
        per_device, mesh=mesh, in_specs=in_specs, out_specs=out_specs, check_vma=False
    )
```

```python
import math

import jax
import jax.numpy as jnp
import ml_dtypes
import numpy as np
from jax import lax
from jax.experimental import pallas as pl
from jax.experimental.pallas import tpu as pltpu
from jax.sharding import PartitionSpec as P

W = 32
APOD = 64
GROUP = 8
LANES = 128


HBM = pl.BlockSpec(memory_space=pltpu.HBM)
VMEM = pl.BlockSpec(memory_space=pltpu.VMEM)
SMEM = pl.BlockSpec(memory_space=pltpu.SMEM)
BF16 = jnp.bfloat16
F32 = jnp.float32


def trig(frequencies, samples, length):
    phase = (frequencies[:, None] * samples[None, :]) % length
    angle = phase * (2.0 * math.pi / length)
    return np.cos(angle), np.sin(angle)


def row_tables(length, devices):
    half = length // 2
    parts = half // (2 * GROUP * devices)
    both = np.stack(trig(np.arange(half), np.arange(half), length))
    both = both.reshape(2, parts, devices, GROUP, 2, half)
    both = both.transpose(1, 4, 2, 0, 3, 5)
    return both.reshape(parts, 2, devices, 2 * GROUP, half).astype(ml_dtypes.bfloat16)


def column_tables(length):
    half = length // 2
    quarter = half // 2
    unit = quarter // 8
    out = []
    for parity in range(2):
        cos_part, sin_part = trig(np.arange(half), 2 * np.arange(quarter) + parity, length)
        spans = [(0, 4 * unit), (4 * unit, 6 * unit), (6 * unit, 7 * unit), (7 * unit, 8 * unit)]
        out.append(np.concatenate(
            [part[:, lo:hi] for lo, hi in spans for part in (cos_part, sin_part)], axis=1
        ))
    return np.stack(out).astype(ml_dtypes.bfloat16)


def part_widths(length, devices):
    half = length // 2
    rows = 2 * GROUP * devices
    widths = []
    for start in range(0, half, rows):
        widest = math.isqrt((half - 1) ** 2 - 1 - start * start) if start < half - 1 else 0
        units = widest // (half // 8) + 1
        widths.append(next(w for w in (4, 6, 7, 8) if w >= units))
    return widths


def pair_index(first, second, count):
    low = jnp.minimum(first, second)
    high = jnp.maximum(first, second)
    return low * count - (low * (low - 1)) // 2 + high - low


def edge_position(edge_squared, rows_squared):
    gap = jnp.maximum(edge_squared - rows_squared, 0)
    root = jnp.sqrt(gap.astype(F32)).astype(jnp.int32)
    for _ in range(2):
        root = jnp.where(root * root < gap, root + 1, root)
    for _ in range(2):
        less = root - 1
        root = jnp.where((less >= 0) & (less * less >= gap), less, root)
    return root


def gather_kernel(maps, swap, mine, same, cross, sems):
    length = maps.shape[2]
    here = lax.axis_index("freq")
    other = 1 - here
    copies = [
        pltpu.make_async_copy(maps.at[0, other], swap, sems.at[0]),
        pltpu.make_async_copy(maps.at[0, here], mine, sems.at[1]),
    ]
    for side, start in enumerate((0, length - W)):
        rows = pl.ds(start, W)
        copies.append(
            pltpu.make_async_copy(maps.at[0, here, rows], same.at[side], sems.at[2 + side])
        )
        copies.append(
            pltpu.make_async_copy(maps.at[0, other, rows], cross.at[side], sems.at[4 + side])
        )
    for copy in copies:
        copy.start()
    for copy in copies:
        copy.wait()


def transform(tables, widths, folded, margin, select, columns, cols, outs, sign, zbins, freqs):
    z_at = lax.axis_index("zbin")
    f_at = lax.axis_index("freq")
    devices = zbins * freqs
    half = folded.shape[1]
    summed = []
    for parity in range(2):
        blocks = []
        for table in tables:
            for rel in range(devices):
                to_z = lax.rem(z_at + rel // freqs, zbins)
                to_f = lax.rem(f_at + rel % freqs, freqs)
                blocks.append(table[parity, to_z * freqs + to_f])
        left = jnp.concatenate(blocks, axis=0)
        picked = jnp.dot(left, select[parity], preferred_element_type=F32).astype(BF16)
        total = jnp.dot(left, folded[parity], preferred_element_type=F32)
        summed.append(total + jnp.dot(picked, margin[...], preferred_element_type=F32))
    for part in range(len(tables) * devices * 2):
        both = jnp.concatenate([v[part * GROUP : (part + 1) * GROUP] for v in summed], axis=0)
        here = slice(part * 2 * GROUP, (part + 1) * 2 * GROUP)
        cols[0, here, :] = both[:, :half].astype(BF16)
        cols[1, here, :] = (both[:, half:] * sign).astype(BF16)
    products = [
        jnp.dot(cols[parity], columns[parity], preferred_element_type=F32) for parity in range(2)
    ]
    left_half = lax.broadcasted_iota(jnp.int32, (2 * GROUP, LANES), 1) < LANES // 2
    for index in range(len(tables) * devices * 2):
        table, rest = divmod(index, devices * 2)
        rel, kind = divmod(rest, 2)
        out = outs[rel]
        here = slice(index * 2 * GROUP, (index + 1) * 2 * GROUP)
        even, odd = [
            [v[here, block * LANES : (block + 1) * LANES] for block in range(4)] for v in products
        ]
        width = widths[table]
        placed = [even[0], even[1], odd[0], odd[1], even[2], odd[2]]
        if width == 7:
            placed.append(jnp.where(left_half, even[3], pltpu.roll(odd[3], LANES // 2, axis=1)))
        placed += [even[3], odd[3]]
        start = sum(widths[:table])
        for block in range(width):
            lanes = slice((start + block) * LANES, (start + block + 1) * LANES)
            out[kind, :, lanes] = placed[block].astype(BF16)


def taper_at(position, length):
    distance = jnp.minimum(position, length - 1 - position)
    ramp = 0.5 - 0.5 * jnp.cos(math.pi * (distance.astype(F32) + 0.5) / APOD)
    return jnp.where(distance < APOD, ramp, 1.0)


def fold_kernel(
    kmax, mine, theirs, source_rows, edges, folded, select, col_taper, below, counts
):
    f_at = lax.axis_index("freq")
    p_at = lax.axis_index("patch")
    length, half = mine.shape
    quarter = half // 2
    place = lax.broadcasted_iota(jnp.int32, (1, half), 1)
    taper_mine = taper_at(place + f_at * half, length)
    taper_theirs = taper_at(place + (1 - f_at) * half, length)
    col_taper[0:1, :] = taper_mine
    col_taper[1:2, :] = taper_theirs
    rows = 2 * GROUP

    def fold_rows(start, top_taper, low_taper):
        pieces = []
        for offset, taper in ((start, top_taper), (start + half, low_taper)):
            near = mine[pl.ds(offset, rows), :].astype(F32) * taper_mine
            far = theirs[pl.ds(offset, rows), :].astype(F32) * taper_theirs
            if taper is not None:
                near = near * taper
                far = far * taper
            pieces.append((near + far, near - far))
        (top_even, top_odd), (low_even, low_odd) = pieces
        here = pl.ds(start, rows)
        folded[0, here, :half] = (top_even + low_even).astype(BF16)
        folded[0, here, half:] = (top_odd + low_odd).astype(BF16)
        folded[1, here, :half] = (top_even - low_even).astype(BF16)
        folded[1, here, half:] = (top_odd - low_odd).astype(BF16)

    def row_weight(start):
        at = start + lax.broadcasted_iota(jnp.int32, (rows, LANES), 0)
        return jnp.tile(taper_at(at, length), (1, half // LANES))

    for block in range(APOD // rows):
        start = block * rows
        fold_rows(start, row_weight(start), None)
        start = half - APOD + block * rows
        fold_rows(start, None, row_weight(start + half))

    def inner(block, carry):
        fold_rows(pl.multiple_of(block * rows, rows), None, None)
        return carry

    lax.fori_loop(APOD // rows, (half - APOD) // rows, inner, 0)

    lane = lax.broadcasted_iota(jnp.int32, (1, kmax * W), 1)
    entry = lane // W
    target = lane - entry * W
    for k in range(kmax):
        target = target + jnp.where(entry == k, source_rows[p_at, k], 0)
    lower = target >= half
    folded_target = jnp.where(lower, target - half, target)
    sample = lax.broadcasted_iota(jnp.int32, (half, kmax * W), 0)
    hit = sample == folded_target
    select[0] = jnp.where(hit, 1.0, 0.0).astype(BF16)
    select[1] = jnp.where(hit, jnp.where(lower, -1.0, 1.0), 0.0).astype(BF16)

    unit = LANES // 4
    at = lax.broadcasted_iota(jnp.int32, (LANES, half), 0)
    limit = lax.broadcasted_iota(jnp.int32, (LANES, half), 1)
    split = at // (2 * unit)
    narrow = quarter - 2 * unit + lax.rem(at, unit)
    sizes = [
        2 * at, 2 * at + 1,
        2 * (LANES + lax.rem(at, 2 * unit)), 2 * (LANES + lax.rem(at, 2 * unit)) + 1,
        2 * (narrow + unit * split), 2 * (narrow + unit * split) + 1,
        2 * narrow + split,
    ]
    for block, size in enumerate(sizes):
        weight = jnp.where(size < limit, jnp.where(size == 0, 1.0, 2.0), 0.0)
        below[block * LANES : (block + 1) * LANES, :] = weight.astype(BF16)

    edge = edges[...]
    bands = edge.shape[1]
    wave = lax.broadcasted_iota(jnp.int32, (half, bands), 0)
    position = edge_position(edge * edge, wave * wave)
    inside_row = jnp.where(position > 0, 2 * position - 1, 0).astype(F32)
    below_edge = jnp.sum(inside_row, axis=0, keepdims=True)
    previous = pltpu.roll(jnp.broadcast_to(below_edge, (8, bands)), 1, axis=1)
    first = lax.broadcasted_iota(jnp.int32, (8, bands), 1) == 0
    counts[...] = (below_edge - jnp.where(first, 1.0, previous)) * float(length * length)


def first_kernel(zbins, freqs, kmax, widths, *refs):
    (folded, select, col_taper, left_same, right_same, left_cross, right_cross, source_ids,
     source_rows, source_counts, row_table, columns) = refs[:12]
    devices = zbins * freqs
    outs = refs[12 : 12 + devices]
    margin, strips, cols = refs[12 + devices :]
    f_at = lax.axis_index("freq")
    p_at = lax.axis_index("patch")
    half = folded.shape[1]
    length = 2 * half
    strips[0, 0:2] = left_same[...]
    strips[0, 2:4] = right_same[...]
    strips[1, 0:2] = left_cross[...]
    strips[1, 2:4] = right_cross[...]
    sign = jnp.where(f_at == 0, 1.0, -1.0).astype(F32)
    for k in range(kmax):
        strip = source_ids[p_at, k]
        near_pair = strip // 2 == p_at + 1 - 2 * lax.rem(p_at, 2)
        slot = jnp.where(near_pair, 0, 2) + lax.rem(strip, 2)
        live = jnp.where(k < source_counts[p_at], 1.0, 0.0).astype(F32)
        position = source_rows[p_at, k] + lax.broadcasted_iota(jnp.int32, (W, LANES), 0)
        weight = jnp.tile(taper_at(position, length) * live, (1, half // LANES))
        near = strips[0, slot].astype(F32) * col_taper[0:1, :] * weight
        far = strips[1, slot].astype(F32) * col_taper[1:2, :] * weight
        here = slice(k * W, (k + 1) * W)
        margin[here, :half] = (near + far).astype(BF16)
        margin[here, half:] = (near - far).astype(BF16)
    tables = [row_table.at[part] for part in range(len(widths))]
    transform(tables, widths, folded, margin, select, columns, cols, outs, sign, zbins, freqs)


def later_kernel(zbins, freqs, groups, *refs):
    row_table, columns, folded, margin, select = refs[:5]
    devices = zbins * freqs
    outs, cols = refs[5:-1], refs[-1]
    sign = jnp.where(lax.axis_index("freq") == 0, 1.0, -1.0).astype(F32)
    start = 0
    for number, widths in enumerate(groups):
        tables = [row_table.at[start + part] for part in range(len(widths))]
        start += len(widths)
        transform(
            tables, widths, folded, margin, select, columns, cols.at[number],
            outs[number * devices : (number + 1) * devices], sign, zbins, freqs,
        )


def band_kernel(zbins, freqs, first_part, widths, last, per, *refs):
    devices = zbins * freqs
    edges, below = refs[:2]
    modes = refs[2 : 2 + devices]
    rest = refs[2 + devices :]
    earlier = None
    if first_part > 0:
        earlier, rest = rest[0], rest[1:]
    if last:
        counts, bank, class_id = rest[:3]
        results, rest = rest[3 : 3 + devices], rest[3 + devices :]
        running, placed, terms = rest
    else:
        running, terms = rest
    z_at = lax.axis_index("zbin")
    f_at = lax.axis_index("freq")
    own = z_at * freqs + f_at
    half = below.shape[1]
    rows = 2 * GROUP
    bands = edges.shape[1]
    edge = edges[...]
    pairs = [(a, b) for a in range(devices) for b in range(a, devices)]
    height = len(pairs) * rows
    totals = [None] * len(pairs)
    start = 0
    for part, width in enumerate(widths):
        spans = [(0, 1), (2, 3), (4,), (5,), (6,), (7,)]
        spans = [span for span in spans if span[-1] < width]
        kept = [0, 1, 2, 3, 4, 5] if width == 8 else [0, 1, 2, 3, 6]
        kept = kept[: len(spans)]
        for column, span in enumerate(spans):
            loaded = []
            for block in span:
                lanes = slice((start + block) * LANES, (start + block + 1) * LANES)
                loaded += [[m[kind, :, lanes].astype(F32) for m in modes] for kind in range(2)]
            for number, (a, b) in enumerate(pairs):
                total = loaded[0][a] * loaded[0][b]
                for values in loaded[1:]:
                    total = total + values[a] * values[b]
                if first_part + part == 0 and column == 0:
                    zero = (
                        (lax.broadcasted_iota(jnp.int32, (rows, LANES), 0) == 0)
                        & (lax.broadcasted_iota(jnp.int32, (rows, LANES), 1) == 0)
                        & (own == 0)
                    )
                    total = jnp.where(zero, 0.0, total)
                high = total.astype(BF16)
                low = (total - high.astype(F32)).astype(BF16)
                lanes = slice(column * LANES, (column + 1) * LANES)
                terms[number * rows : (number + 1) * rows, lanes] = high
                terms[height + number * rows : height + (number + 1) * rows, lanes] = low
        start += width
        used = len(spans)
        if kept == list(range(used)):
            weights = below[: used * LANES, :]
        else:
            weights = jnp.concatenate(
                [below[k * LANES : (k + 1) * LANES, :] for k in kept], axis=0
            )
        sums = jnp.dot(terms[:, : used * LANES], weights, preferred_element_type=F32)
        sums = sums[:height] + sums[height:]
        row_at = lax.broadcasted_iota(jnp.int32, (rows, bands), 0)
        within = jnp.where(row_at < GROUP, 2 * row_at, 2 * (row_at - GROUP) + 1)
        ky = ((first_part + part) * devices + own) * rows + within
        place = edge_position(edge * edge, ky * ky)
        tile = place // LANES
        inside = place - tile * LANES
        for number in range(len(pairs)):
            here = slice(number * rows, (number + 1) * rows)
            chosen = jnp.zeros((rows, bands), F32)
            for block in range(half // LANES):
                moved = jnp.take_along_axis(
                    sums[here, block * LANES : (block + 1) * LANES], inside, axis=1
                )
                chosen = jnp.where(tile == block, moved, chosen)
            added = jnp.sum(chosen.reshape(rows // 8, 8, bands), axis=0)
            totals[number] = added if totals[number] is None else totals[number] + added
    for number in range(len(pairs)):
        running[number] = (
            totals[number] if earlier is None else totals[number] + earlier[number]
        )
    if last:
        first_np, second_np = np.triu_indices(devices)

        def place_of(number):
            source = int(number)
            rel_z = lax.rem(z_at - source // freqs + zbins, zbins)
            rel_f = lax.rem(f_at - source % freqs + freqs, freqs)
            return rel_z * freqs + rel_f

        for number in range(len(pairs)):
            low = place_of(first_np[number])
            high = place_of(second_np[number])
            row = jnp.sum(running[pair_index(low, high, devices)], axis=0, keepdims=True)
            placed[pl.ds(number, 1), :] = row
        total = placed[...]
        first = lax.broadcasted_iota(jnp.int32, total.shape, 1) == 0
        total = total - jnp.where(first, 0.0, pltpu.roll(total, 1, axis=1))
        pseudo = total / counts[0:1, :]
        p_at = lax.axis_index("patch")
        spectra = lax.dot_general(
            pseudo, bank[class_id[p_at] ^ p_at], (((1,), (1,)), ((), ())),
            precision=lax.Precision.HIGHEST, preferred_element_type=F32,
        )
        placed[...] = spectra
        for rel in range(devices):
            to_z = lax.rem(z_at + rel // freqs, zbins)
            for number in range(per):
                results[rel][number] = placed[pl.ds(to_z * per + number, 1), :]


def per_device(
    density_maps, margin_src, margin_row, margin_count, class_id, coupling_bank, band_edges
):
    patch_local, bins_local, length, columns = density_maps.shape
    freqs = lax.axis_size("freq")
    zbins = lax.axis_size("zbin")
    patches = lax.axis_size("patch")
    devices = zbins * freqs
    half = length // 2
    kmax = margin_src.shape[1]
    bands = band_edges.shape[0] - 1
    rows = 2 * GROUP
    assert patch_local == 1 and bins_local == freqs == 2 and columns == half == 4 * LANES
    assert patches & (patches - 1) == 0 and bands == LANES
    pairs = devices * (devices + 1) // 2
    per = pairs // zbins
    padded = -(-pairs // 8) * 8
    widths = part_widths(length, devices)
    share = len(widths) // 4
    groups = [widths[at : at + share] for at in range(0, len(widths), share)]
    shape = jax.ShapeDtypeStruct

    def limit(megabytes):
        return pltpu.CompilerParams(vmem_limit_bytes=megabytes << 20)

    swap, mine, same, cross = pl.pallas_call(
        gather_kernel,
        in_specs=[HBM],
        out_specs=[VMEM] * 4,
        out_shape=[shape((length, columns), BF16)] * 2 + [shape((2, W, columns), BF16)] * 2,
        scratch_shapes=[pltpu.SemaphoreType.DMA((6,))],
        compiler_params=limit(6),
        name="gather",
    )(density_maps)
    matchings = [
        [(p, (p - 1 + 2 * (p % 2)) % patches) for p in range(patches)],
        [(p, p ^ 1) for p in range(patches)],
    ]
    arrived = []
    for hops in matchings:
        crossed = [(a * freqs + f, b * freqs + 1 - f) for a, b in hops for f in range(freqs)]
        arrived.append(lax.ppermute(same, "patch", hops))
        arrived.append(lax.ppermute(cross, ("patch", "freq"), crossed))
    right_same, right_cross, left_same, left_cross = arrived
    theirs = lax.ppermute(swap, "freq", [(0, 1), (1, 0)])

    upper_edges = band_edges[1:].reshape(1, bands)
    folded, select, col_taper, below, counts = pl.pallas_call(
        lambda *refs: fold_kernel(kmax, *refs),
        in_specs=[VMEM, VMEM, SMEM, VMEM],
        out_specs=[VMEM] * 5,
        out_shape=[
            shape((2, half, length), BF16), shape((2, half, kmax * W), BF16),
            shape((2, half), F32), shape((7 * LANES, half), BF16), shape((8, bands), F32),
        ],
        compiler_params=limit(12),
        name="fold",
    )(mine, theirs, margin_row, upper_edges)

    row_table = row_tables(length, devices)
    first_table, later_table = jnp.asarray(row_table[:share]), jnp.asarray(row_table[share:])
    column_table = jnp.asarray(column_tables(length))

    def pieces_of(group):
        return [shape((2, rows, sum(group) * LANES), BF16)] * devices

    result = pl.pallas_call(
        lambda *refs: first_kernel(zbins, freqs, kmax, groups[0], *refs),
        in_specs=[VMEM] * 7 + [SMEM] * 3 + [VMEM] * 2,
        out_specs=[VMEM] * (devices + 1),
        out_shape=pieces_of(groups[0]) + [shape((kmax * W, length), BF16)],
        scratch_shapes=[
            pltpu.VMEM((2, 4, W, half), BF16),
            pltpu.VMEM((2, 2 * share * devices * rows, half), BF16),
        ],
        compiler_params=limit(20),
        name="first",
    )(
        folded, select, col_taper, left_same, right_same, left_cross, right_cross, margin_src,
        margin_row, margin_count, first_table, column_table,
    )
    pieces = [result[:devices]]
    margin = result[devices]
    later = pl.pallas_call(
        lambda *refs: later_kernel(zbins, freqs, groups[1:], *refs),
        in_specs=[VMEM] * 5,
        out_specs=[VMEM] * (devices * (len(groups) - 1)),
        out_shape=[piece for group in groups[1:] for piece in pieces_of(group)],
        scratch_shapes=[
            pltpu.VMEM((len(groups) - 1, 2, 2 * share * devices * rows, half), BF16)
        ],
        compiler_params=limit(24),
        name="later",
    )(later_table, column_table, folded, margin, select)
    for number in range(len(groups) - 1):
        pieces.append(later[number * devices : (number + 1) * devices])

    hops = []
    for rel in range(devices):
        hops.append([
            (z * freqs + f,
             (z + rel // freqs) % zbins * freqs + (f + rel % freqs) % freqs)
            for z in range(zbins) for f in range(freqs)
        ])
    order = list(range(freqs, devices)) + list(range(1, freqs))

    def exchange(arrays):
        got = {0: arrays[0]}
        for rel in order:
            got[rel] = lax.ppermute(arrays[rel], ("zbin", "freq"), hops[rel])
        return [got[rel] for rel in range(devices)]

    received = [exchange(group) for group in pieces]
    running = None
    for number, group in enumerate(groups):
        last = number == len(groups) - 1
        arrays = [upper_edges, below] + received[number] + ([running] if number > 0 else [])
        specs = [VMEM] * len(arrays)
        scratch = [pltpu.VMEM((2 * pairs * rows, 6 * LANES), BF16)]
        sums = (pairs, 8, bands)
        if last:
            arrays += [counts, bank, class_id]
            specs += [VMEM, VMEM, SMEM]
            out_shape = [shape((per, 1, bands), F32)] * devices
            scratch = [pltpu.VMEM(sums, F32), pltpu.VMEM((padded, bands), F32)] + scratch
        else:
            out_shape = [shape(sums, F32)]
        got = pl.pallas_call(
            lambda *refs, number=number, group=group, last=last: band_kernel(
                zbins, freqs, number * share, group, last, per, *refs
            ),
            in_specs=specs,
            out_specs=[VMEM] * len(out_shape),
            out_shape=out_shape,
            scratch_shapes=scratch,
            compiler_params=limit(8),
            name="bands" + str(number),
        )(*arrays)
        if not last:
            running = got[0]
        if number == 0:
            bank, running = lax.optimization_barrier((coupling_bank, running))
            step = 1
            while step < patches:
                swapped = lax.ppermute(bank, "patch", [(i, i ^ step) for i in range(patches)])
                bank = jnp.concatenate([bank, swapped], axis=0)
                step *= 2
    parts = exchange(got)
    total = parts[0]
    for part in parts[1:]:
        total = total + part
    return total.reshape(patch_local, per, bands)


def solution(mesh):
    in_specs = (
        P(("groups", "patch"), "zbin", None, "freq"),
        P("groups", None),
        P("groups", None),
        P("groups"),
        P("groups"),
        P("patch", None, None),
        P(),
    )
    out_specs = P(("groups", "patch"), "zbin", None)
    return jax.shard_map(
        per_device, mesh=mesh, in_specs=in_specs, out_specs=out_specs, check_vma=False
    )
```

```python
import math

import jax
import jax.numpy as jnp
import ml_dtypes
import numpy as np
from jax import lax
from jax.experimental import pallas as pl
from jax.experimental.pallas import tpu as pltpu
from jax.sharding import PartitionSpec as P


W = 32
APOD = 64
GROUP = 8
LANES = 128


HBM = pl.BlockSpec(memory_space=pltpu.HBM)
VMEM = pl.BlockSpec(memory_space=pltpu.VMEM)
SMEM = pl.BlockSpec(memory_space=pltpu.SMEM)
BF16 = jnp.bfloat16
F32 = jnp.float32


def trig(frequencies, samples, length):
    phase = (frequencies[:, None] * samples[None, :]) % length
    angle = phase * (2.0 * math.pi / length)
    return np.cos(angle), np.sin(angle)


def row_tables(length, devices):
    half = length // 2
    parts = half // (2 * GROUP * devices)
    both = np.stack(trig(np.arange(half), np.arange(half), length))
    both = both.reshape(2, parts, devices, GROUP, 2, half)
    both = both.transpose(1, 4, 2, 0, 3, 5)
    return both.reshape(parts, 2, devices, 2 * GROUP, half).astype(ml_dtypes.bfloat16)


def column_tables(length):
    half = length // 2
    quarter = half // 2
    unit = quarter // 8
    out = []
    for parity in range(2):
        cos_part, sin_part = trig(np.arange(half), 2 * np.arange(quarter) + parity, length)
        spans = [(0, 4 * unit), (4 * unit, 6 * unit), (6 * unit, 7 * unit), (7 * unit, 8 * unit)]
        out.append(np.concatenate(
            [part[:, lo:hi] for lo, hi in spans for part in (cos_part, sin_part)], axis=1
        ))
    return np.stack(out).astype(ml_dtypes.bfloat16)


def part_widths(length, devices):
    half = length // 2
    rows = 2 * GROUP * devices
    widths = []
    for start in range(0, half, rows):
        widest = math.isqrt((half - 1) ** 2 - 1 - start * start) if start < half - 1 else 0
        units = widest // (half // 8) + 1
        widths.append(next(w for w in (4, 6, 7, 8) if w >= units))
    return widths


def pair_index(first, second, count):
    low = jnp.minimum(first, second)
    high = jnp.maximum(first, second)
    return low * count - (low * (low - 1)) // 2 + high - low


def edge_position(edge_squared, rows_squared):
    gap = jnp.maximum(edge_squared - rows_squared, 0)
    root = jnp.sqrt(gap.astype(F32)).astype(jnp.int32)
    for _ in range(2):
        root = jnp.where(root * root < gap, root + 1, root)
    for _ in range(2):
        less = root - 1
        root = jnp.where((less >= 0) & (less * less >= gap), less, root)
    return root


def strips_kernel(maps, same, cross, sems):
    length = maps.shape[2]
    here = lax.axis_index("freq")
    copies = []
    for side, start in enumerate((0, length - W)):
        rows = pl.ds(start, W)
        copies.append(
            pltpu.make_async_copy(maps.at[0, here, rows], same.at[side], sems.at[side])
        )
        copies.append(
            pltpu.make_async_copy(maps.at[0, 1 - here, rows], cross.at[side], sems.at[2 + side])
        )
    for copy in copies:
        copy.start()
    for copy in copies:
        copy.wait()


def gather_kernel(maps, swap, mine, sems):
    here = lax.axis_index("freq")
    copies = [
        pltpu.make_async_copy(maps.at[0, 1 - here], swap, sems.at[0]),
        pltpu.make_async_copy(maps.at[0, here], mine, sems.at[1]),
    ]
    for copy in copies:
        copy.start()
    for copy in copies:
        copy.wait()


def transform(tables, widths, folded, margin, select, columns, cols, outs, sign, zbins, freqs):
    z_at = lax.axis_index("zbin")
    f_at = lax.axis_index("freq")
    devices = zbins * freqs
    half = folded.shape[1]
    summed = []
    for parity in range(2):
        blocks = []
        for table in tables:
            for rel in range(devices):
                to_z = lax.rem(z_at + rel // freqs, zbins)
                to_f = lax.rem(f_at + rel % freqs, freqs)
                blocks.append(table[parity, to_z * freqs + to_f])
        left = jnp.concatenate(blocks, axis=0)
        picked = jnp.dot(left, select[parity], preferred_element_type=F32).astype(BF16)
        total = jnp.dot(left, folded[parity], preferred_element_type=F32)
        summed.append(total + jnp.dot(picked, margin[...], preferred_element_type=F32))
    for part in range(len(tables) * devices * 2):
        both = jnp.concatenate([v[part * GROUP : (part + 1) * GROUP] for v in summed], axis=0)
        here = slice(part * 2 * GROUP, (part + 1) * 2 * GROUP)
        cols[0, here, :] = both[:, :half].astype(BF16)
        cols[1, here, :] = (both[:, half:] * sign).astype(BF16)
    products = [
        jnp.dot(cols[parity], columns[parity], preferred_element_type=F32) for parity in range(2)
    ]
    left_half = lax.broadcasted_iota(jnp.int32, (2 * GROUP, LANES), 1) < LANES // 2
    for index in range(len(tables) * devices * 2):
        table, rest = divmod(index, devices * 2)
        rel, kind = divmod(rest, 2)
        out = outs[rel]
        here = slice(index * 2 * GROUP, (index + 1) * 2 * GROUP)
        even, odd = [
            [v[here, block * LANES : (block + 1) * LANES] for block in range(4)] for v in products
        ]
        width = widths[table]
        placed = [even[0], even[1], odd[0], odd[1], even[2], odd[2]]
        if width == 7:
            placed.append(jnp.where(left_half, even[3], pltpu.roll(odd[3], LANES // 2, axis=1)))
        placed += [even[3], odd[3]]
        start = sum(widths[:table])
        for block in range(width):
            lanes = slice((start + block) * LANES, (start + block + 1) * LANES)
            out[kind, :, lanes] = placed[block].astype(BF16)


def taper_at(position, length):
    distance = jnp.minimum(position, length - 1 - position)
    ramp = 0.5 - 0.5 * jnp.cos(math.pi * (distance.astype(F32) + 0.5) / APOD)
    return jnp.where(distance < APOD, ramp, 1.0)


def fold_kernel(kmax, mine, theirs, source_rows, folded, select, col_taper):
    f_at = lax.axis_index("freq")
    p_at = lax.axis_index("patch")
    length, half = mine.shape
    place = lax.broadcasted_iota(jnp.int32, (1, half), 1)
    taper_mine = taper_at(place + f_at * half, length)
    taper_theirs = taper_at(place + (1 - f_at) * half, length)
    col_taper[0:1, :] = taper_mine
    col_taper[1:2, :] = taper_theirs
    rows = 2 * GROUP

    def fold_rows(start, top_taper, low_taper):
        pieces = []
        for offset, taper in ((start, top_taper), (start + half, low_taper)):
            near = mine[pl.ds(offset, rows), :].astype(F32) * taper_mine
            far = theirs[pl.ds(offset, rows), :].astype(F32) * taper_theirs
            if taper is not None:
                near = near * taper
                far = far * taper
            pieces.append((near + far, near - far))
        (top_even, top_odd), (low_even, low_odd) = pieces
        here = pl.ds(start, rows)
        folded[0, here, :half] = (top_even + low_even).astype(BF16)
        folded[0, here, half:] = (top_odd + low_odd).astype(BF16)
        folded[1, here, :half] = (top_even - low_even).astype(BF16)
        folded[1, here, half:] = (top_odd - low_odd).astype(BF16)

    def row_weight(start):
        at = start + lax.broadcasted_iota(jnp.int32, (rows, LANES), 0)
        return jnp.tile(taper_at(at, length), (1, half // LANES))

    for block in range(APOD // rows):
        start = block * rows
        fold_rows(start, row_weight(start), None)
        start = half - APOD + block * rows
        fold_rows(start, None, row_weight(start + half))

    def inner(block, carry):
        fold_rows(pl.multiple_of(block * rows, rows), None, None)
        return carry

    lax.fori_loop(APOD // rows, (half - APOD) // rows, inner, 0)

    lane = lax.broadcasted_iota(jnp.int32, (1, kmax * W), 1)
    entry = lane // W
    target = lane - entry * W
    for k in range(kmax):
        target = target + jnp.where(entry == k, source_rows[p_at, k], 0)
    lower = target >= half
    folded_target = jnp.where(lower, target - half, target)
    sample = lax.broadcasted_iota(jnp.int32, (half, kmax * W), 0)
    hit = sample == folded_target
    select[0] = jnp.where(hit, 1.0, 0.0).astype(BF16)
    select[1] = jnp.where(hit, jnp.where(lower, -1.0, 1.0), 0.0).astype(BF16)


def bands_setup_kernel(edges, below, counts):
    half = below.shape[1]
    quarter = half // 2
    unit = LANES // 4
    at = lax.broadcasted_iota(jnp.int32, (LANES, half), 0)
    limit = lax.broadcasted_iota(jnp.int32, (LANES, half), 1)
    split = at // (2 * unit)
    narrow = quarter - 2 * unit + lax.rem(at, unit)
    sizes = [
        2 * at, 2 * at + 1,
        2 * (LANES + lax.rem(at, 2 * unit)), 2 * (LANES + lax.rem(at, 2 * unit)) + 1,
        2 * (narrow + unit * split), 2 * (narrow + unit * split) + 1,
        2 * narrow + split,
    ]
    for block, size in enumerate(sizes):
        weight = jnp.where(size < limit, jnp.where(size == 0, 1.0, 2.0), 0.0)
        below[block * LANES : (block + 1) * LANES, :] = weight.astype(BF16)

    edge = edges[...]
    bands = edge.shape[1]
    wave = lax.broadcasted_iota(jnp.int32, (half, bands), 0)
    position = edge_position(edge * edge, wave * wave)
    inside_row = jnp.where(position > 0, 2 * position - 1, 0).astype(F32)
    below_edge = jnp.sum(inside_row, axis=0, keepdims=True)
    previous = pltpu.roll(jnp.broadcast_to(below_edge, (8, bands)), 1, axis=1)
    first = lax.broadcasted_iota(jnp.int32, (8, bands), 1) == 0
    counts[...] = (below_edge - jnp.where(first, 1.0, previous)) * float(4 * half * half)


def first_kernel(zbins, freqs, kmax, widths, *refs):
    (folded, select, col_taper, left_same, right_same, left_cross, right_cross, source_ids,
     source_rows, source_counts, row_table, columns) = refs[:12]
    devices = zbins * freqs
    outs = refs[12 : 12 + devices]
    margin, strips, cols = refs[12 + devices :]
    f_at = lax.axis_index("freq")
    p_at = lax.axis_index("patch")
    half = folded.shape[1]
    length = 2 * half
    strips[0, 0:2] = left_same[...]
    strips[0, 2:4] = right_same[...]
    strips[1, 0:2] = left_cross[...]
    strips[1, 2:4] = right_cross[...]
    sign = jnp.where(f_at == 0, 1.0, -1.0).astype(F32)
    for k in range(kmax):
        strip = source_ids[p_at, k]
        near_pair = strip // 2 == p_at + 1 - 2 * lax.rem(p_at, 2)
        slot = jnp.where(near_pair, 0, 2) + lax.rem(strip, 2)
        live = jnp.where(k < source_counts[p_at], 1.0, 0.0).astype(F32)
        position = source_rows[p_at, k] + lax.broadcasted_iota(jnp.int32, (W, LANES), 0)
        weight = jnp.tile(taper_at(position, length) * live, (1, half // LANES))
        near = strips[0, slot].astype(F32) * col_taper[0:1, :] * weight
        far = strips[1, slot].astype(F32) * col_taper[1:2, :] * weight
        here = slice(k * W, (k + 1) * W)
        margin[here, :half] = (near + far).astype(BF16)
        margin[here, half:] = (near - far).astype(BF16)
    tables = [row_table.at[part] for part in range(len(widths))]
    transform(tables, widths, folded, margin, select, columns, cols, outs, sign, zbins, freqs)


def later_kernel(zbins, freqs, groups, *refs):
    row_table, columns, folded, margin, select = refs[:5]
    devices = zbins * freqs
    outs, cols = refs[5:-1], refs[-1]
    sign = jnp.where(lax.axis_index("freq") == 0, 1.0, -1.0).astype(F32)
    start = 0
    for number, widths in enumerate(groups):
        tables = [row_table.at[start + part] for part in range(len(widths))]
        start += len(widths)
        transform(
            tables, widths, folded, margin, select, columns, cols.at[number],
            outs[number * devices : (number + 1) * devices], sign, zbins, freqs,
        )


def band_kernel(zbins, freqs, first_part, widths, last, per, *refs):
    devices = zbins * freqs
    edges, below = refs[:2]
    modes = refs[2 : 2 + devices]
    rest = refs[2 + devices :]
    earlier = None
    if first_part > 0:
        earlier, rest = rest[0], rest[1:]
    if last:
        counts, bank, class_id = rest[:3]
        results, rest = rest[3 : 3 + devices], rest[3 + devices :]
        running, placed, terms = rest
    else:
        running, terms = rest
    z_at = lax.axis_index("zbin")
    f_at = lax.axis_index("freq")
    own = z_at * freqs + f_at
    half = below.shape[1]
    rows = 2 * GROUP
    bands = edges.shape[1]
    edge = edges[...]
    pairs = [(a, b) for a in range(devices) for b in range(a, devices)]
    height = len(pairs) * rows
    totals = [None] * len(pairs)
    start = 0
    for part, width in enumerate(widths):
        spans = [(0, 1), (2, 3), (4,), (5,), (6,), (7,)]
        spans = [span for span in spans if span[-1] < width]
        kept = [0, 1, 2, 3, 4, 5] if width == 8 else [0, 1, 2, 3, 6]
        kept = kept[: len(spans)]
        for column, span in enumerate(spans):
            loaded = []
            for block in span:
                lanes = slice((start + block) * LANES, (start + block + 1) * LANES)
                loaded += [[m[kind, :, lanes].astype(F32) for m in modes] for kind in range(2)]
            for number, (a, b) in enumerate(pairs):
                total = loaded[0][a] * loaded[0][b]
                for values in loaded[1:]:
                    total = total + values[a] * values[b]
                if first_part + part == 0 and column == 0:
                    zero = (
                        (lax.broadcasted_iota(jnp.int32, (rows, LANES), 0) == 0)
                        & (lax.broadcasted_iota(jnp.int32, (rows, LANES), 1) == 0)
                        & (own == 0)
                    )
                    total = jnp.where(zero, 0.0, total)
                high = total.astype(BF16)
                low = (total - high.astype(F32)).astype(BF16)
                lanes = slice(column * LANES, (column + 1) * LANES)
                terms[number * rows : (number + 1) * rows, lanes] = high
                terms[height + number * rows : height + (number + 1) * rows, lanes] = low
        start += width
        used = len(spans)
        if kept == list(range(used)):
            weights = below[: used * LANES, :]
        else:
            weights = jnp.concatenate(
                [below[k * LANES : (k + 1) * LANES, :] for k in kept], axis=0
            )
        sums = jnp.dot(terms[:, : used * LANES], weights, preferred_element_type=F32)
        sums = sums[:height] + sums[height:]
        row_at = lax.broadcasted_iota(jnp.int32, (rows, bands), 0)
        within = jnp.where(row_at < GROUP, 2 * row_at, 2 * (row_at - GROUP) + 1)
        ky = ((first_part + part) * devices + own) * rows + within
        place = edge_position(edge * edge, ky * ky)
        tile = place // LANES
        inside = place - tile * LANES
        for number in range(len(pairs)):
            here = slice(number * rows, (number + 1) * rows)
            chosen = jnp.zeros((rows, bands), F32)
            for block in range(half // LANES):
                moved = jnp.take_along_axis(
                    sums[here, block * LANES : (block + 1) * LANES], inside, axis=1
                )
                chosen = jnp.where(tile == block, moved, chosen)
            added = jnp.sum(chosen.reshape(rows // 8, 8, bands), axis=0)
            totals[number] = added if totals[number] is None else totals[number] + added
    for number in range(len(pairs)):
        running[number] = (
            totals[number] if earlier is None else totals[number] + earlier[number]
        )
    if last:
        first_np, second_np = np.triu_indices(devices)

        def place_of(number):
            source = int(number)
            rel_z = lax.rem(z_at - source // freqs + zbins, zbins)
            rel_f = lax.rem(f_at - source % freqs + freqs, freqs)
            return rel_z * freqs + rel_f

        for number in range(len(pairs)):
            low = place_of(first_np[number])
            high = place_of(second_np[number])
            row = jnp.sum(running[pair_index(low, high, devices)], axis=0, keepdims=True)
            placed[pl.ds(number, 1), :] = row
        total = placed[...]
        first = lax.broadcasted_iota(jnp.int32, total.shape, 1) == 0
        total = total - jnp.where(first, 0.0, pltpu.roll(total, 1, axis=1))
        pseudo = total / counts[0:1, :]
        p_at = lax.axis_index("patch")
        spectra = lax.dot_general(
            pseudo, bank[class_id[p_at] ^ p_at], (((1,), (1,)), ((), ())),
            precision=lax.Precision.HIGHEST, preferred_element_type=F32,
        )
        placed[...] = spectra
        for rel in range(devices):
            to_z = lax.rem(z_at + rel // freqs, zbins)
            for number in range(per):
                results[rel][number] = placed[pl.ds(to_z * per + number, 1), :]


def per_device(
    density_maps, margin_src, margin_row, margin_count, class_id, coupling_bank, band_edges
):
    patch_local, bins_local, length, columns = density_maps.shape
    freqs = lax.axis_size("freq")
    zbins = lax.axis_size("zbin")
    patches = lax.axis_size("patch")
    devices = zbins * freqs
    half = length // 2
    kmax = margin_src.shape[1]
    bands = band_edges.shape[0] - 1
    rows = 2 * GROUP
    assert patch_local == 1 and bins_local == freqs == 2 and columns == half == 4 * LANES
    assert patches & (patches - 1) == 0 and bands == LANES
    pairs = devices * (devices + 1) // 2
    per = pairs // zbins
    padded = -(-pairs // 8) * 8
    widths = part_widths(length, devices)
    share = len(widths) // 4
    groups = [widths[at : at + share] for at in range(0, len(widths), share)]
    shape = jax.ShapeDtypeStruct

    def limit(megabytes):
        return pltpu.CompilerParams(vmem_limit_bytes=megabytes << 20)

    density_maps = pltpu.with_memory_space_constraint(density_maps, pltpu.HBM)
    same, cross = pl.pallas_call(
        strips_kernel,
        in_specs=[HBM],
        out_specs=[VMEM] * 2,
        out_shape=[shape((2, W, columns), BF16)] * 2,
        scratch_shapes=[pltpu.SemaphoreType.DMA((4,))],
        compiler_params=limit(2),
        name="strips",
    )(density_maps)
    swap, mine = pl.pallas_call(
        gather_kernel,
        in_specs=[HBM],
        out_specs=[VMEM] * 2,
        out_shape=[shape((length, columns), BF16)] * 2,
        scratch_shapes=[pltpu.SemaphoreType.DMA((2,))],
        compiler_params=limit(6),
        name="gather",
    )(density_maps)
    matchings = [
        [(p, (p - 1 + 2 * (p % 2)) % patches) for p in range(patches)],
        [(p, p ^ 1) for p in range(patches)],
    ]
    arrived = []
    for hops in matchings:
        crossed = [(a * freqs + f, b * freqs + 1 - f) for a, b in hops for f in range(freqs)]
        arrived.append(lax.ppermute(same, "patch", hops))
        arrived.append(lax.ppermute(cross, ("patch", "freq"), crossed))
    right_same, right_cross, left_same, left_cross = arrived
    theirs = lax.ppermute(swap, "freq", [(0, 1), (1, 0)])

    folded, select, col_taper = pl.pallas_call(
        lambda *refs: fold_kernel(kmax, *refs),
        in_specs=[VMEM, VMEM, SMEM],
        out_specs=[VMEM] * 3,
        out_shape=[
            shape((2, half, length), BF16), shape((2, half, kmax * W), BF16),
            shape((2, half), F32),
        ],
        compiler_params=limit(12),
        name="fold",
    )(mine, theirs, margin_row)

    row_table = row_tables(length, devices)
    first_table, later_table = jnp.asarray(row_table[:share]), jnp.asarray(row_table[share:])
    column_table = jnp.asarray(column_tables(length))

    def pieces_of(group):
        return [shape((2, rows, sum(group) * LANES), BF16)] * devices

    result = pl.pallas_call(
        lambda *refs: first_kernel(zbins, freqs, kmax, groups[0], *refs),
        in_specs=[VMEM] * 7 + [SMEM] * 3 + [VMEM] * 2,
        out_specs=[VMEM] * (devices + 1),
        out_shape=pieces_of(groups[0]) + [shape((kmax * W, length), BF16)],
        scratch_shapes=[
            pltpu.VMEM((2, 4, W, half), BF16),
            pltpu.VMEM((2, 2 * share * devices * rows, half), BF16),
        ],
        compiler_params=limit(20),
        name="first",
    )(
        folded, select, col_taper, left_same, right_same, left_cross, right_cross, margin_src,
        margin_row, margin_count, first_table, column_table,
    )
    pieces = [result[:devices]]
    margin = result[devices]
    later = pl.pallas_call(
        lambda *refs: later_kernel(zbins, freqs, groups[1:], *refs),
        in_specs=[VMEM] * 5,
        out_specs=[VMEM] * (devices * (len(groups) - 1)),
        out_shape=[piece for group in groups[1:] for piece in pieces_of(group)],
        scratch_shapes=[
            pltpu.VMEM((len(groups) - 1, 2, 2 * share * devices * rows, half), BF16)
        ],
        compiler_params=limit(24),
        name="later",
    )(later_table, column_table, folded, margin, select)
    for number in range(len(groups) - 1):
        pieces.append(later[number * devices : (number + 1) * devices])

    hops = []
    for rel in range(devices):
        hops.append([
            (z * freqs + f,
             (z + rel // freqs) % zbins * freqs + (f + rel % freqs) % freqs)
            for z in range(zbins) for f in range(freqs)
        ])
    order = list(range(freqs, devices)) + list(range(1, freqs))

    def exchange(arrays):
        got = {0: arrays[0]}
        for rel in order:
            got[rel] = lax.ppermute(arrays[rel], ("zbin", "freq"), hops[rel])
        return [got[rel] for rel in range(devices)]

    received = [exchange(group) for group in pieces]
    upper_edges = band_edges[1:].reshape(1, bands)
    below, counts = pl.pallas_call(
        bands_setup_kernel,
        in_specs=[VMEM],
        out_specs=[VMEM] * 2,
        out_shape=[shape((7 * LANES, half), BF16), shape((8, bands), F32)],
        compiler_params=limit(6),
        name="setup",
    )(upper_edges)
    running = None
    for number, group in enumerate(groups):
        last = number == len(groups) - 1
        arrays = [upper_edges, below] + received[number] + ([running] if number > 0 else [])
        specs = [VMEM] * len(arrays)
        scratch = [pltpu.VMEM((2 * pairs * rows, 6 * LANES), BF16)]
        sums = (pairs, 8, bands)
        if last:
            arrays += [counts, bank, class_id]
            specs += [VMEM, VMEM, SMEM]
            out_shape = [shape((per, 1, bands), F32)] * devices
            scratch = [pltpu.VMEM(sums, F32), pltpu.VMEM((padded, bands), F32)] + scratch
        else:
            out_shape = [shape(sums, F32)]
        got = pl.pallas_call(
            lambda *refs, number=number, group=group, last=last: band_kernel(
                zbins, freqs, number * share, group, last, per, *refs
            ),
            in_specs=specs,
            out_specs=[VMEM] * len(out_shape),
            out_shape=out_shape,
            scratch_shapes=scratch,
            compiler_params=limit(8),
        )(*arrays)
        if not last:
            running = got[0]
        if number == 0:
            bank = coupling_bank
            step = 1
            while step < patches:
                swapped = lax.ppermute(bank, "patch", [(i, i ^ step) for i in range(patches)])
                bank = jnp.concatenate([bank, swapped], axis=0)
                step *= 2
    parts = exchange(got)
    total = parts[0]
    for part in parts[1:]:
        total = total + part
    return total.reshape(patch_local, per, bands)


def solution(mesh):
    in_specs = (
        P(("groups", "patch"), "zbin", None, "freq"),
        P("groups", None),
        P("groups", None),
        P("groups"),
        P("groups"),
        P("patch", None, None),
        P(),
    )
    out_specs = P(("groups", "patch"), "zbin", None)
    return jax.shard_map(
        per_device, mesh=mesh, in_specs=in_specs, out_specs=out_specs, check_vma=False
    )
```
